128 devices in a mesh: seq: 64 (over x_hi, z, y, core), tensor: 2 (over x_lo).
Axes of the slice: x: 4 (x_hi: 2, x_lo: 2; x = x_hi * 2 + x_lo), y: 4, z: 4, core: 2. Of those that a mesh axis runs over, the one named last changes fastest.
Arguments:
- hidden: bfloat16 [4096, 7168], P('seq', 'tensor'), may hold values from -200 to 200
- attn_gain: float32 [7168], P('tensor'), may hold values from 0.25 to 1.75
- kv_down: bfloat16 [7168, 576], P('tensor'), may hold values from -0.0625 to 0.0625
- kv_gain: float32 [512], replicated, may hold values from 0.25 to 1.75
- q_nope: bfloat16 [4096, 16384], P('seq', 'tensor'), may hold values from -90 to 90
- q_pe: bfloat16 [4096, 8192], P('seq', 'tensor'), may hold values from -6 to 6
- w_uk: bfloat16 [128, 128, 512], P('tensor'), may hold values from -0.5 to 0.5
- w_uv: bfloat16 [128, 512, 128], P('tensor'), may hold values from -1 to 1
- doc_ids: int32 [4096], replicated, may hold values from 0 to 3, never falling along the last dimension, each value on 1 to 3072 neighbouring positions
- slot_table: int32 [256], replicated, may hold values from 0 to 255, each once
Outputs:
- attn_values: bfloat16 [4096, 16384], P('seq', 'tensor')
- latent_cache: bfloat16 [4096, 576], P('seq')
The draws below stay inside these ranges and needn't reach their ends.
Inputs may be any that keep to these rules, and one draw needn't show every extreme that they name: `doc_ids`: 4 documents packed in order, the longest exactly 3072 tokens. `slot_table`: each cache slot receives exactly one token block.
All inputs are finite; a program needn't handle non-finite values.
Results may differ from the reference program's by a relative error of at most 0.0093.
Values may be sent and summed in bfloat16 or wider, within the bound.
No kernel may reach another device: no remote copies, remote signals or barrier semaphores. Data moves between devices by JAX's collectives and lax.ppermute only.
A program may use at most 128 MiB of HBM per device.

```python
import functools
import math
import jax
import jax.numpy as jnp
import numpy as np
from jax import lax

D = 7168
HEADS = 128
LATENT = 512
ROPE = 64
NOPE = 128
VD = 128
BLOCK = 16
DOCS = 4
TOKENS = 4096


def draw_hidden(key, part):
    scale_key, column_key, entry_key = jax.random.split(jax.random.fold_in(key, 11), 3)
    row_scale = jnp.exp(jax.random.uniform(scale_key, (TOKENS, 1), jnp.float32, 0.0, math.log(10.0)))
    column_ramp = (1.0 + 2.5 * jnp.arange(D, dtype=jnp.float32) / D)[None, :]
    column_scale = column_ramp * jnp.exp(jax.random.uniform(column_key, (1, D), jnp.float32, -0.5, 0.5))
    gaussian = jax.random.normal(entry_key, (TOKENS, D), jnp.float32)
    return jnp.clip(gaussian * row_scale * column_scale, -200.0, 200.0).astype(jnp.bfloat16)


def draw_q_nope(key, part):
    entry_key = jax.random.fold_in(jax.random.fold_in(key, 23), 0)
    values = jnp.clip(jax.random.normal(entry_key, (TOKENS, HEADS * NOPE), jnp.float32), -6.0, 6.0)
    return values.astype(jnp.bfloat16)


def level_of(stream_key, dims, shards, least, largest):
    level, own = 1.0, jax.random.fold_in(stream_key, 6)
    for position, blocks in shards:
        heights = jnp.exp(jax.random.uniform(jax.random.fold_in(own, position), (blocks,), jnp.float32, least / len(shards), largest / len(shards)))
        level = level * jnp.repeat(heights, dims[position] // blocks).reshape([-1 if axis == position else 1 for axis in range(len(dims))])
    return level


def profile(amount, total, most, skew):
    weights = [(1 << 20) // math.isqrt(standing ** skew) + 1 for standing in range(2, amount + 1)]
    spare, counts = total - most - (amount - 1), [1] * (amount - 1)
    while spare > 0:
        candidates = [i for i in range(amount - 1) if counts[i] < most]
        mass, remaining = sum([weights[i] for i in candidates]), spare
        for i in candidates:
            more = min(most - counts[i], max(1, remaining * weights[i] // mass), spare)
            counts[i] = counts[i] + more
            spare = spare - more
    return np.array([most] + counts)


def ragged_sizes(rng, number_of, total, most, slope):
    if number_of == 2:
        one = jax.random.randint(rng, (), max(1, total - most), min(most, total - 1) + 1)
        return jnp.stack([one, total - one])
    tallies = jnp.asarray(profile(number_of, total, most, slope), jnp.int32)
    pairs = (number_of - 1) // 2
    source_of, taker = tallies[1:1 + 2 * pairs:2], tallies[2:2 + 2 * pairs:2]
    room = jnp.minimum(source_of - 1, most - taker)
    moved = jax.random.randint(jax.random.fold_in(rng, 1), (pairs,), 0, 1 << 20) % (room + 1)
    tallies = tallies.at[1:1 + 2 * pairs:2].set(source_of - moved).at[2:2 + 2 * pairs:2].set(taker + moved)
    return tallies[jax.random.permutation(jax.random.fold_in(rng, 2), number_of)]


def noise(own_key, dims, scale, bound, pieces=(), kind=jnp.bfloat16):
    array = scale * jax.random.normal(own_key, dims, jnp.float32)
    if pieces:
        array = array * level_of(own_key, dims, pieces, -0.22, 0.18)
    return jnp.clip(array, -bound, bound).astype(kind)


def setup_inputs(seed: int = 0) -> dict:
    splits = jax.random.split(jax.random.key(seed), 11)
    return {
        "hidden": draw_hidden(jax.random.fold_in(splits[10], 71), 0),
        "attn_gain": jnp.clip(1.0 + 0.15 * jax.random.normal(splits[1], (D,), jnp.float32), 0.25, 1.75),
        "kv_down": noise(splits[2], (D, LATENT + ROPE), D ** -0.5, 0.0625, ((0, 2),)),
        "kv_gain": jnp.clip(1.0 + 0.15 * jax.random.normal(splits[3], (LATENT,), jnp.float32), 0.25, 1.75),
        "q_nope": draw_q_nope(jax.random.fold_in(splits[10], 71), 0),
        "q_pe": noise(splits[5], (TOKENS, HEADS * ROPE), 1.0, 6.0, ((0, 64), (1, 2))),
        "w_uk": noise(splits[6], (HEADS, NOPE, LATENT), NOPE ** -0.5, 0.5, ((0, 2),)),
        "w_uv": noise(splits[7], (HEADS, LATENT, VD), (LATENT // 16) ** -0.5, 1.0, ((0, 2),)),
        "doc_ids": jnp.searchsorted(jnp.cumsum(ragged_sizes(splits[8], DOCS, TOKENS, TOKENS * 3 // 4, 0)), jnp.arange(TOKENS), side="right").astype(jnp.int32),
        "slot_table": jax.random.permutation(splits[9], TOKENS // BLOCK).astype(jnp.int32),
    }


EPSILON = 1e-06
MASKED = -1e+30

def rounded(value):
    return lax.optimization_barrier(value.astype(jnp.bfloat16))

def block_rows(total_rows):
    block_size = min(total_rows, 512)
    while total_rows % block_size:
        block_size -= 1
    return block_size

def angles(positions, width):
    middle = width // 2
    frequency = jnp.exp(jnp.arange(middle, dtype=jnp.float32) * (-2.0 * math.log(10000.0) / width))
    angle_table = positions[:, None] * frequency[None, :]
    return (jnp.cos(angle_table), jnp.sin(angle_table))

def rotate(values, cosine_part, sine_part):
    middle = values.shape[-1] // 2
    first_half = values[..., :middle]
    second_half = values[..., middle:]
    return jnp.concatenate([first_half * cosine_part - second_half * sine_part, second_half * cosine_part + first_half * sine_part], axis=-1)

def finish(projected, squares, positions, kv_gain):
    scaled = projected * lax.rsqrt(squares / D + EPSILON)[:, None]
    raw_latent = scaled[:, :LATENT]
    raw_key = scaled[:, LATENT:]
    latent = (raw_latent * lax.rsqrt(lax.optimization_barrier(jnp.mean(raw_latent * raw_latent, axis=1, keepdims=True)) + EPSILON) * kv_gain).astype(jnp.bfloat16)
    cosine_part, sine_part = angles(positions.astype(jnp.float32), raw_key.shape[1])
    return (latent, rotate(raw_key, cosine_part, sine_part).astype(jnp.bfloat16))

def attend_group(inputs, keys_latent, keys_rope, allowed):
    nope_group, rope_group, down_keys, up_values = inputs
    highest = lax.Precision.HIGHEST
    query_latent = rounded(jnp.einsum('thd,hdc->thc', nope_group.astype(jnp.float32), down_keys.astype(jnp.float32), precision=highest)).astype(jnp.float32)
    scores = jnp.einsum('thc,uc->thu', query_latent, keys_latent.astype(jnp.float32), precision=highest)
    scores = scores + jnp.einsum('thr,ur->thu', rope_group.astype(jnp.float32), keys_rope.astype(jnp.float32), precision=highest)
    scores = scores * (NOPE + ROPE) ** (-0.5)
    scores = jnp.where(allowed[:, None, :], scores, MASKED)
    top_score = lax.optimization_barrier(jnp.max(scores, axis=2, keepdims=True))
    weights = jnp.where(allowed[:, None, :], jnp.exp(scores - top_score), 0.0)
    denominator = lax.optimization_barrier(jnp.sum(weights, axis=2, keepdims=True))
    weighted = jnp.einsum('thu,uc->thc', rounded(weights).astype(jnp.float32), keys_latent.astype(jnp.float32), precision=highest)
    mixed = rounded(weighted / denominator).astype(jnp.float32)
    return jnp.einsum('thc,hcv->thv', mixed, up_values.astype(jnp.float32), precision=highest).astype(jnp.bfloat16)

def reference(hidden, attn_gain, kv_down, kv_gain, q_nope, q_pe, w_uk, w_uv, doc_ids, slot_table):
    widened = hidden.astype(jnp.float32)
    squares = lax.optimization_barrier(jnp.sum(widened * widened, axis=1))
    normed_in = (widened * attn_gain).astype(jnp.bfloat16)
    projected = jnp.dot(normed_in, kv_down, preferred_element_type=jnp.float32)
    positions = jnp.arange(TOKENS, dtype=jnp.int32)
    latent, key_rope = finish(projected, squares, positions, kv_gain)
    cosine_part, sine_part = angles(positions.astype(jnp.float32), ROPE)
    query_rope = rotate(q_pe.astype(jnp.float32).reshape(TOKENS, HEADS, ROPE), cosine_part[:, None, :], sine_part[:, None, :]).astype(jnp.bfloat16)
    query_rows = block_rows(TOKENS)
    group = 16 if HEADS % 16 == 0 else HEADS
    groups = HEADS // group
    down_groups = w_uk.reshape(groups, group, NOPE, LATENT)
    up_groups = w_uv.reshape(groups, group, LATENT, VD)
    outputs = []
    for block_index in range(TOKENS // query_rows):
        begin = block_index * query_rows
        end = begin + query_rows
        allowed = (positions[None, :end] <= positions[begin:end, None]) & (doc_ids[None, :end] == doc_ids[begin:end, None])
        nope_part = q_nope[begin:end].reshape(query_rows, groups, group, NOPE).transpose(1, 0, 2, 3)
        rope_part = query_rope[begin:end].reshape(query_rows, groups, group, ROPE).transpose(1, 0, 2, 3)
        attend = functools.partial(attend_group, keys_latent=latent[:end], keys_rope=key_rope[:end], allowed=allowed)
        result = lax.map(attend, (nope_part, rope_part, down_groups, up_groups))
        outputs.append(result.transpose(1, 0, 2, 3).reshape(query_rows, HEADS * VD))
    attn_values = jnp.concatenate(outputs, axis=0)
    blocks = jnp.concatenate([latent, key_rope], axis=1).reshape(TOKENS // BLOCK, BLOCK, LATENT + ROPE)
    latent_cache = jnp.zeros_like(blocks).at[slot_table].set(blocks).reshape(TOKENS, LATENT + ROPE)
    return (attn_values, latent_cache)
```

```python
import functools
import math

import jax
import jax.numpy as jnp
from jax import lax
from jax.experimental import pallas as pl
from jax.experimental.pallas import tpu as pltpu
from jax.sharding import PartitionSpec as P

D = 7168
HEADS = 128
LATENT = 512
ROPE = 64
NOPE = 128
VD = 128
BLOCK = 16
WIDTH = 640

EPSILON = 1e-06
MASKED = -1e30
FLOOR = -1e20
SCALE = (NOPE + ROPE) ** (-0.5) * math.log2(math.e)

ROWS = 64
GROUP = 8
STEP = 256


def params(**kw):
    return pltpu.CompilerParams(vmem_limit_bytes=56 << 20, **kw)


def swap_halves(x, lane):
    return jnp.where(
        (lane & 63) < 32, pltpu.roll(x, 96, axis=1), pltpu.roll(x, 32, axis=1)
    )


def project_kernel(hidden_ref, gain_ref, down_ref, out_ref):
    k = pl.program_id(0)

    @pl.when(k == 0)
    def _():
        out_ref[...] = jnp.zeros_like(out_ref)

    widened = hidden_ref[...].astype(jnp.float32)
    normed = (widened * gain_ref[...]).astype(jnp.bfloat16)
    product = jnp.dot(normed, down_ref[...], preferred_element_type=jnp.float32)
    out_ref[:, : LATENT + ROPE] += product
    squares = jnp.sum(widened * widened, axis=1, keepdims=True)
    out_ref[:, LATENT + ROPE :] += jnp.broadcast_to(squares, (ROWS, WIDTH - LATENT - ROPE))


def project(hidden, attn_gain, kv_down):
    width = hidden.shape[1]
    tile = width // 7
    return pl.pallas_call(
        project_kernel,
        out_shape=jax.ShapeDtypeStruct((ROWS, WIDTH), jnp.float32),
        grid=(7,),
        in_specs=[
            pl.BlockSpec((ROWS, tile), lambda k: (0, k)),
            pl.BlockSpec((1, tile), lambda k: (0, k)),
            pl.BlockSpec((tile, LATENT + ROPE), lambda k: (k, 0)),
        ],
        out_specs=pl.BlockSpec((ROWS, WIDTH), lambda k: (0, 0)),
        compiler_params=params(dimension_semantics=("arbitrary",)),
        name="project",
    )(hidden, attn_gain.reshape(1, -1), kv_down)


def finish_kernel(mine_ref, theirs_ref, cos_ref, sin_ref, gain_ref, out_ref):
    total = mine_ref[...] + theirs_ref[...]
    squares = total[:, WIDTH - 1 :]
    scaled = total * lax.rsqrt(squares / D + EPSILON)
    raw = scaled[:, :LATENT]
    mean = jnp.mean(raw * raw, axis=1, keepdims=True)
    latent = raw * lax.rsqrt(mean + EPSILON) * gain_ref[...]
    out_ref[:, :LATENT] = latent.astype(jnp.bfloat16)
    key = scaled[:, LATENT:]
    lane = lax.broadcasted_iota(jnp.int32, key.shape, 1)
    key = jnp.where(lane < ROPE, key, pltpu.roll(key, ROPE, axis=1))
    turned = key * cos_ref[...] + swap_halves(key, lane) * sin_ref[...]
    out_ref[:, LATENT:] = turned.astype(jnp.bfloat16)


def finish(mine, theirs, cosines, sines, kv_gain):
    return pl.pallas_call(
        finish_kernel,
        out_shape=jax.ShapeDtypeStruct((ROWS, WIDTH), jnp.bfloat16),
        compiler_params=params(),
        name="finish",
    )(mine, theirs, cosines, sines, kv_gain.reshape(1, -1))


def queries_kernel(nope_ref, pe_ref, cos_ref, sin_ref, uk_ref, out_ref):
    lane = lax.broadcasted_iota(jnp.int32, (ROWS, 128), 1)
    for pair in range(GROUP // 2):
        pe = pe_ref[:, pair * 128 : (pair + 1) * 128].astype(jnp.float32)
        turned = pe * cos_ref[...] + swap_halves(pe, lane) * sin_ref[...]
        for side in range(2):
            head = 2 * pair + side
            rows = slice(head * ROWS, (head + 1) * ROWS)
            keep = (lane < ROPE) if side == 0 else (lane >= ROPE)
            out_ref[rows, LATENT:] = jnp.where(keep, turned, 0.0).astype(jnp.bfloat16)
            out_ref[rows, :LATENT] = jnp.dot(
                nope_ref[:, head * NOPE : (head + 1) * NOPE],
                uk_ref[head],
                preferred_element_type=jnp.float32,
            ).astype(jnp.bfloat16)


def make_queries(q_nope, q_pe, cosines, sines, w_uk):
    heads = w_uk.shape[0]
    return pl.pallas_call(
        queries_kernel,
        out_shape=jax.ShapeDtypeStruct((heads * ROWS, WIDTH), jnp.bfloat16),
        grid=(heads // GROUP,),
        in_specs=[
            pl.BlockSpec((ROWS, GROUP * NOPE), lambda g: (0, g)),
            pl.BlockSpec((ROWS, GROUP * ROPE), lambda g: (0, g)),
            pl.BlockSpec((ROWS, 128), lambda g: (0, 0)),
            pl.BlockSpec((ROWS, 128), lambda g: (0, 0)),
            pl.BlockSpec((GROUP, NOPE, LATENT), lambda g: (g, 0, 0)),
        ],
        out_specs=pl.BlockSpec((GROUP * ROWS, WIDTH), lambda g: (g, 0)),
        compiler_params=params(dimension_semantics=("arbitrary",)),
        name="queries",
    )(q_nope, q_pe, cosines, sines, w_uk)


def start_of(scalars, position):
    start = jnp.int32(0)
    for i in range(3):
        start = jnp.maximum(start, jnp.where(scalars[i] <= position, scalars[i], 0))
    return start


def attend_kernel(offsets, first, last, *refs):
    n = len(offsets)
    refs = list(refs)
    scalars = refs.pop(0)
    q_ref = refs.pop(0)
    sets = [refs.pop(0) for _ in range(n)]
    if last:
        uv_ref = refs.pop(0)
    if not first:
        acc_in, m_in, l_in = refs[:3]
        refs = refs[3:]
    if last:
        out_ref = refs.pop(0)
        kv, ids, counts, acc, m, l = refs
    else:
        acc, m, l = refs[:3]
        kv, ids, counts = refs[3:]
    me = scalars[3]

    @pl.when(pl.program_id(0) == 0)
    def _():
        x, z, y, c = me // 32, (me // 8) & 3, (me // 2) & 3, me & 1
        lowest = start_of(scalars, me * ROWS)
        highest = start_of(scalars, me * ROWS + ROWS - 1)
        counts[0] = 0
        for want_whole in (True, False):
            for a, (dy, dc) in enumerate(offsets):
                for b in range(8):
                    dz, dx = b // 2, b % 2
                    block = (
                        (x ^ dx) * 32 + ((z + dz) & 3) * 8 + ((y + dy) & 3) * 2 + (c ^ dc)
                    )
                    whole = (block < me) & (block * ROWS >= highest)
                    needed = (block <= me) & (block * ROWS + ROWS - 1 >= lowest)
                    take = whole if want_whole else (needed & jnp.logical_not(whole))

                    @pl.when(take)
                    def _(a=a, b=b, block=block):
                        at = counts[0]
                        ids[at] = block
                        kv[pl.ds(pl.multiple_of(at * ROWS, ROWS), ROWS), :] = sets[a][
                            b * ROWS : (b + 1) * ROWS, :
                        ]
                        counts[0] = at + 1

            if want_whole:
                counts[1] = counts[0] // 4
        found = counts[0]
        for i in range(3):
            ids[found + i] = HEADS * 1024
            kv[pl.ds(pl.multiple_of((found + i) * ROWS, ROWS), ROWS), :] = jnp.zeros(
                (ROWS, WIDTH), jnp.bfloat16
            )
        counts[2] = (found + 3) // 4

    if first:
        acc[...] = jnp.zeros_like(acc)
        m[...] = jnp.full_like(m, FLOOR)
        l[...] = jnp.zeros_like(l)
    else:
        acc[...] = acc_in[...]
        m[...] = m_in[...]
        l[...] = l_in[...]

    sub = 256

    def step(j, masked):
        keys = kv[pl.ds(pl.multiple_of(j * STEP, STEP), STEP), :]
        if masked:
            lane = lax.broadcasted_iota(jnp.int32, (sub, STEP), 1)
            key_block = jnp.where(
                lane < 128,
                jnp.where(lane < 64, ids[4 * j], ids[4 * j + 1]),
                jnp.where(lane < 192, ids[4 * j + 2], ids[4 * j + 3]),
            )
            key_position = key_block * ROWS + (lane & 63)
            row = lax.broadcasted_iota(jnp.int32, (sub, STEP), 0)
            position = me * ROWS + (row & 63)
            allowed = (key_position <= position) & (
                key_position >= start_of(scalars, position)
            )
        for r in range(GROUP * ROWS // sub):
            rows = slice(r * sub, (r + 1) * sub)
            scores = lax.dot_general(
                q_ref[rows, :], keys, (((1,), (1,)), ((), ())), preferred_element_type=jnp.float32
            )
            if masked:
                scores = jnp.where(allowed, scores, MASKED)
            m_old = m[rows, :]
            m_new = jnp.maximum(m_old, jnp.max(scores, axis=1, keepdims=True))
            weights = jnp.exp2((scores - jnp.tile(m_new, (1, STEP // 128))) * SCALE)
            factor = jnp.exp2((m_old - m_new) * SCALE)
            l[rows, :] = l[rows, :] * factor + (weights[:, :128] + weights[:, 128:])
            m[rows, :] = m_new
            acc[rows, :] = acc[rows, :] * jnp.tile(factor, (1, LATENT // 128)) + jnp.dot(
                weights.astype(jnp.bfloat16), keys[:, :LATENT], preferred_element_type=jnp.float32
            )

    def whole(j, carry):
        step(j, False)
        return carry

    def partial(j, carry):
        step(j, True)
        return carry

    lax.fori_loop(0, counts[1], whole, 0)
    lax.fori_loop(counts[1], counts[2], partial, 0)

    if last:
        for head in range(GROUP):
            rows = slice(head * ROWS, (head + 1) * ROWS)
            total = jnp.sum(l[rows, :], axis=1, keepdims=True)
            mixed = (acc[rows, :] / total).astype(jnp.bfloat16)
            out_ref[:, head * VD : (head + 1) * VD] = jnp.dot(
                mixed, uv_ref[head], preferred_element_type=jnp.float32
            ).astype(jnp.bfloat16)


def attend(scalars, queries, sets, offsets, state, w_uv):
    first, last = state is None, w_uv is not None
    n = len(sets)
    rows = GROUP * ROWS
    total = queries.shape[0]
    by_group = lambda width: pl.BlockSpec((rows, width), lambda g, s: (g, 0))
    in_specs = [by_group(WIDTH)] + [
        pl.BlockSpec((8 * ROWS, WIDTH), lambda g, s: (0, 0)) for _ in sets
    ]
    operands = [queries, *sets]
    if last:
        in_specs.append(pl.BlockSpec((GROUP, LATENT, VD), lambda g, s: (g, 0, 0)))
        operands.append(w_uv)
    widths = (LATENT, 128, 128)
    aliases = {}
    if not first:
        in_specs += [by_group(w) for w in widths]
        operands += list(state)
    scratch = [
        pltpu.VMEM(((8 * n + 4) * ROWS, WIDTH), jnp.bfloat16),
        pltpu.SMEM((8 * n + 4,), jnp.int32),
        pltpu.SMEM((4,), jnp.int32),
    ]
    if last:
        out_shape = jax.ShapeDtypeStruct((ROWS, total // ROWS * VD), jnp.bfloat16)
        out_specs = pl.BlockSpec((ROWS, GROUP * VD), lambda g, s: (0, g))
        scratch += [pltpu.VMEM((rows, w), jnp.float32) for w in widths]
    else:
        out_shape = [jax.ShapeDtypeStruct((total, w), jnp.float32) for w in widths]
        out_specs = [by_group(w) for w in widths]
    flops = 2 * total * 8 * n * ROWS * (WIDTH + LATENT)
    return pl.pallas_call(
        functools.partial(attend_kernel, offsets, first, last),
        out_shape=out_shape,
        grid_spec=pltpu.PrefetchScalarGridSpec(
            num_scalar_prefetch=1,
            grid=(total // rows,),
            in_specs=in_specs,
            out_specs=out_specs,
            scratch_shapes=scratch,
        ),
        compiler_params=params(dimension_semantics=("arbitrary",)),
        cost_estimate=pl.CostEstimate(
            flops=flops, transcendentals=total * 8 * n * ROWS, bytes_accessed=24 << 20
        ),
        name=f"attend{n}{int(first)}{int(last)}",
    )(scalars, *operands)


def cache_kernel(scalars, *refs):
    sets, (out_ref, buffer, sems) = refs[:8], refs[8:]
    me = scalars[3]
    x, z, y, c = me // 32, (me // 8) & 3, (me // 2) & 3, me & 1
    for slot in range(ROWS // BLOCK):
        group = scalars[4 + slot]
        block = group // 4
        dx, dz = (block // 32) ^ x, ((block // 8) - z) & 3
        dy, dc = ((block // 2) - y) & 3, (block & 1) ^ c
        row = (dz * 2 + dx) * ROWS + (group & 3) * BLOCK
        which = dc * 4 + dy
        for a in range(8):

            @pl.when(which == a)
            def _(a=a, row=row, slot=slot):
                pltpu.make_async_copy(
                    sets[a].at[pl.ds(pl.multiple_of(row, BLOCK), BLOCK), :],
                    buffer.at[slot * BLOCK : (slot + 1) * BLOCK, :],
                    sems.at[slot],
                ).start()

    for slot in range(ROWS // BLOCK):
        pltpu.make_async_copy(
            sets[0].at[:BLOCK, :],
            buffer.at[slot * BLOCK : (slot + 1) * BLOCK, :],
            sems.at[slot],
        ).wait()
    out_ref[...] = buffer[:, : LATENT + ROPE]


def cache_rows(scalars, sets):
    return pl.pallas_call(
        cache_kernel,
        out_shape=jax.ShapeDtypeStruct((ROWS, LATENT + ROPE), jnp.bfloat16),
        grid_spec=pltpu.PrefetchScalarGridSpec(
            num_scalar_prefetch=1,
            grid=(),
            in_specs=[pl.BlockSpec(memory_space=pl.ANY)] * 8,
            out_specs=pl.BlockSpec(memory_space=pltpu.VMEM),
            scratch_shapes=[
                pltpu.VMEM((ROWS, WIDTH), jnp.bfloat16),
                pltpu.SemaphoreType.DMA((ROWS // BLOCK,)),
            ],
        ),
        compiler_params=params(),
        name="cache_rows",
    )(scalars, *sets)


def shard_of(x, z, y, c):
    return (x % 2) * 32 + (z % 4) * 8 + (y % 4) * 2 + c % 2


def fetch(array, dx=0, dz=0, dy=0, dc=0):
    everyone = [
        (x, z, y, c) for x in range(2) for z in range(4) for y in range(4) for c in range(2)
    ]
    pairs = [
        (shard_of(x + dx, z + dz, y + dy, c + dc), shard_of(x, z, y, c))
        for x, z, y, c in everyone
    ]
    return lax.ppermute(array, "seq", pairs)


def local(hidden, attn_gain, kv_down, kv_gain, q_nope, q_pe, w_uk, w_uv, doc_ids, slot_table):
    me = lax.axis_index("seq")
    positions = (me * ROWS + jnp.arange(ROWS, dtype=jnp.int32)).astype(jnp.float32)
    half = ROPE // 2
    frequency = jnp.exp(jnp.arange(half, dtype=jnp.float32) * (-2.0 * math.log(10000.0) / ROPE))
    angle = positions[:, None] * jnp.tile(frequency, 4)[None, :]
    sign = jnp.where((jnp.arange(128) & 63) < half, -1.0, 1.0).astype(jnp.float32)
    cosines, sines = jnp.cos(angle), jnp.sin(angle) * sign[None, :]

    starts = jnp.sum(
        (doc_ids[None, :] < jnp.arange(1, 4, dtype=jnp.int32)[:, None]).astype(jnp.int32), axis=1
    )
    slots = me * (ROWS // BLOCK) + jnp.arange(ROWS // BLOCK, dtype=jnp.int32)
    groups = jnp.arange(slot_table.shape[0], dtype=jnp.int32)
    held = jnp.sum(jnp.where(slot_table[None, :] == slots[:, None], groups[None, :], 0), axis=1)
    scalars = jnp.concatenate([starts, me[None].astype(jnp.int32), held])

    mine = project(hidden, attn_gain, kv_down)
    theirs = lax.ppermute(mine, "tensor", [(0, 1), (1, 0)])
    queries = make_queries(q_nope, q_pe, cosines, sines, w_uk)
    own = finish(mine, theirs, cosines, sines, kv_gain)

    two = jnp.concatenate([own, fetch(own, dx=1)], axis=0)
    eight = jnp.concatenate([two] + [fetch(two, dz=d) for d in (1, 2, 3)], axis=0)
    across = {0: eight}
    for d in (1, 3, 2):
        across[d] = fetch(eight, dy=d)
    beside = {d: fetch(across[d], dc=1) for d in (0, 1, 3, 2)}

    state = attend(
        scalars, queries, [across[0], beside[0]], [(0, 0), (0, 1)], None, None
    )
    state = attend(
        scalars,
        queries,
        [across[1], across[3], beside[1], beside[3]],
        [(1, 0), (3, 0), (1, 1), (3, 1)],
        state,
        None,
    )
    attn_values = attend(
        scalars, queries, [across[2], beside[2]], [(2, 0), (2, 1)], state, w_uv
    )
    latent_cache = cache_rows(
        scalars, [across[d] for d in range(4)] + [beside[d] for d in range(4)]
    )
    return attn_values, latent_cache


def solution(mesh):
    placed = (
        P("seq", "tensor"),
        P("tensor"),
        P("tensor", None),
        P(),
        P("seq", "tensor"),
        P("seq", "tensor"),
        P("tensor", None, None),
        P("tensor", None, None),
        P(),
        P(),
    )
    return jax.shard_map(
        local,
        mesh=mesh,
        in_specs=placed,
        out_specs=(P("seq", "tensor"), P("seq", None)),
        check_vma=False,
    )
```

```python
import functools
import math

import jax
import jax.numpy as jnp
from jax import lax
from jax.experimental import pallas as pl
from jax.experimental.pallas import tpu as pltpu
from jax.sharding import PartitionSpec as P


D = 7168
HEADS = 128
LATENT = 512
ROPE = 64
NOPE = 128
VD = 128
BLOCK = 16
WIDTH = 640

EPSILON = 1e-06
MASKED = -1e30
FLOOR = -1e20
SCALE = (NOPE + ROPE) ** (-0.5) * math.log2(math.e)

ROWS = 64
GROUP = 8
STEP = 256
PARTS = 7
ATTEND_MIB = 20


def params(mib, **kw):
    return pltpu.CompilerParams(vmem_limit_bytes=mib << 20, **kw)


def swap_halves(x, lane):
    return jnp.where(
        (lane & 63) < 32, pltpu.roll(x, 96, axis=1), pltpu.roll(x, 32, axis=1)
    )


def project_kernel(hidden_ref, gain_ref, down_ref, out_ref):
    k = pl.program_id(0)

    @pl.when(k == 0)
    def _():
        out_ref[...] = jnp.zeros_like(out_ref)

    widened = hidden_ref[...].astype(jnp.float32)
    normed = (widened * gain_ref[...].reshape(1, -1)).astype(jnp.bfloat16)
    product = lax.dot_general(
        normed, down_ref[...], (((1,), (1,)), ((), ())), preferred_element_type=jnp.float32
    )
    out_ref[:, : LATENT + ROPE] += product
    squares = jnp.sum(widened * widened, axis=1, keepdims=True)
    out_ref[:, LATENT + ROPE :] += jnp.broadcast_to(squares, (ROWS, WIDTH - LATENT - ROPE))


def project(hidden, attn_gain, kv_down):
    width = hidden.shape[1]
    tile = width // PARTS
    return pl.pallas_call(
        project_kernel,
        out_shape=jax.ShapeDtypeStruct((ROWS, WIDTH), jnp.float32),
        grid=(PARTS,),
        in_specs=[
            pl.BlockSpec((ROWS, tile), lambda k: (0, k)),
            pl.BlockSpec((tile,), lambda k: (k,)),
            pl.BlockSpec((LATENT + ROPE, tile), lambda k: (0, k)),
        ],
        out_specs=pl.BlockSpec((ROWS, WIDTH), lambda k: (0, 0)),
        compiler_params=params(8, dimension_semantics=("arbitrary",)),
        name="project",
    )(hidden, attn_gain, kv_down.T)


def finish_kernel(mine_ref, theirs_ref, cos_ref, sin_ref, gain_ref, out_ref):
    total = mine_ref[...] + theirs_ref[...]
    squares = total[:, WIDTH - 1 :]
    scaled = total * lax.rsqrt(squares / D + EPSILON)
    raw = scaled[:, :LATENT]
    mean = jnp.mean(raw * raw, axis=1, keepdims=True)
    latent = raw * lax.rsqrt(mean + EPSILON) * gain_ref[...]
    out_ref[:, :LATENT] = latent.astype(jnp.bfloat16)
    key = scaled[:, LATENT:]
    lane = lax.broadcasted_iota(jnp.int32, key.shape, 1)
    key = jnp.where(lane < ROPE, key, pltpu.roll(key, ROPE, axis=1))
    turned = key * cos_ref[...] + swap_halves(key, lane) * sin_ref[...]
    out_ref[:, LATENT:] = turned.astype(jnp.bfloat16)


def finish(mine, theirs, cosines, sines, kv_gain):
    return pl.pallas_call(
        finish_kernel,
        out_shape=jax.ShapeDtypeStruct((ROWS, WIDTH), jnp.bfloat16),
        compiler_params=params(4),
        name="finish",
    )(mine, theirs, cosines, sines, kv_gain.reshape(1, -1))


def queries_kernel(nope_ref, pe_ref, cos_ref, sin_ref, uk_ref, out_ref):
    lane = lax.broadcasted_iota(jnp.int32, (ROWS, 128), 1)
    for pair in range(GROUP // 2):
        pe = pe_ref[:, pair * 128 : (pair + 1) * 128].astype(jnp.float32)
        turned = pe * cos_ref[...] + swap_halves(pe, lane) * sin_ref[...]
        for side in range(2):
            head = 2 * pair + side
            rows = slice(head * ROWS, (head + 1) * ROWS)
            keep = (lane < ROPE) if side == 0 else (lane >= ROPE)
            out_ref[rows, LATENT:] = jnp.where(keep, turned, 0.0).astype(jnp.bfloat16)
            out_ref[rows, :LATENT] = jnp.dot(
                nope_ref[:, head * NOPE : (head + 1) * NOPE],
                uk_ref[head],
                preferred_element_type=jnp.float32,
            ).astype(jnp.bfloat16)


def make_queries(q_nope, q_pe, cosines, sines, w_uk):
    heads = w_uk.shape[0]
    return pl.pallas_call(
        queries_kernel,
        out_shape=jax.ShapeDtypeStruct((heads * ROWS, WIDTH), jnp.bfloat16),
        grid=(heads // GROUP,),
        in_specs=[
            pl.BlockSpec((ROWS, GROUP * NOPE), lambda g: (0, g)),
            pl.BlockSpec((ROWS, GROUP * ROPE), lambda g: (0, g)),
            pl.BlockSpec((ROWS, 128), lambda g: (0, 0)),
            pl.BlockSpec((ROWS, 128), lambda g: (0, 0)),
            pl.BlockSpec((GROUP, NOPE, LATENT), lambda g: (g, 0, 0)),
        ],
        out_specs=pl.BlockSpec((GROUP * ROWS, WIDTH), lambda g: (g, 0)),
        compiler_params=params(16, dimension_semantics=("arbitrary",)),
        name="queries",
    )(q_nope, q_pe, cosines, sines, w_uk)


def start_of(scalars, position):
    start = jnp.int32(0)
    for i in range(3):
        start = jnp.maximum(start, jnp.where(scalars[i] <= position, scalars[i], 0))
    return start


def attend_kernel(offsets, first, last, *refs):
    n = len(offsets)
    refs = list(refs)
    scalars = refs.pop(0)
    q_ref = refs.pop(0)
    sets = [refs.pop(0) for _ in range(n)]
    if last:
        uv_ref = refs.pop(0)
    if not first:
        before, refs = refs[:3], refs[3:]
    if last:
        out_ref = refs.pop(0)
        kv, ids, counts, even, odd, acc, m, l = refs
    else:
        acc, m, l = refs[:3]
        kv, ids, counts, even, odd = refs[3:]
    me = scalars[3]
    blocks = STEP // ROWS
    rows = GROUP * ROWS
    groups = q_ref.shape[0] // rows

    x, z, y, c = me // 32, (me // 8) & 3, (me // 2) & 3, me & 1
    lowest = start_of(scalars, me * ROWS)
    counts[0] = 0
    for a, (dy, dc) in enumerate(offsets):
        for b in range(8):
            dz, dx = b // 2, b % 2
            block = (x ^ dx) * 32 + ((z + dz) & 3) * 8 + ((y + dy) & 3) * 2 + (c ^ dc)
            needed = (block <= me) & (block * ROWS + ROWS - 1 >= lowest)

            @pl.when(needed)
            def _(a=a, b=b, block=block):
                at = counts[0]
                ids[at] = block
                kv[pl.ds(pl.multiple_of(at * ROWS, ROWS), ROWS), :] = sets[a][
                    b * ROWS : (b + 1) * ROWS, :
                ]
                counts[0] = at + 1

    found = counts[0]
    for i in range(blocks - 1):
        ids[found + i] = HEADS * 1024
        kv[pl.ds(pl.multiple_of((found + i) * ROWS, ROWS), ROWS), :] = jnp.zeros(
            (ROWS, WIDTH), jnp.bfloat16
        )
    steps = (found + blocks - 1) // blocks

    def ready(g, carry):
        at = pl.ds(pl.multiple_of(g * rows, rows), rows)
        if first:
            acc[at, :] = jnp.zeros((rows, LATENT), jnp.float32)
            m[at, :] = jnp.full((rows, 128), FLOOR, jnp.float32)
            l[at, :] = jnp.zeros((rows, 128), jnp.float32)
        else:
            for new, old in zip((acc, m, l), before):
                new[at, :] = old[at, :]
        return carry

    lax.fori_loop(0, groups, ready, 0)

    def keys_of(j):
        return kv[pl.ds(pl.multiple_of(j * STEP, STEP), STEP), :]

    def score(g, j, into):
        into[...] = lax.dot_general(
            q_ref[pl.ds(pl.multiple_of(g * rows, rows), rows), :],
            keys_of(j),
            (((1,), (1,)), ((), ())),
            preferred_element_type=jnp.float32,
        )

    def gather(g, j, scores):
        at = pl.ds(pl.multiple_of(g * rows, rows), rows)
        lane = lax.broadcasted_iota(jnp.int32, (ROWS, STEP), 1)
        key_block = jnp.full((ROWS, STEP), ids[blocks * j], jnp.int32)
        for i in range(1, blocks):
            key_block = jnp.where(lane >= i * ROWS, ids[blocks * j + i], key_block)
        key_position = key_block * ROWS + (lane & (ROWS - 1))
        position = me * ROWS + lax.broadcasted_iota(jnp.int32, (ROWS, STEP), 0)
        allowed = (key_position <= position) & (key_position >= start_of(scalars, position))
        s = jnp.where(allowed[None], scores[...].reshape(GROUP, ROWS, STEP), MASKED)
        s = s.reshape(rows, STEP)
        m_old = m[at, :]
        m_new = jnp.maximum(m_old, jnp.max(s, axis=1, keepdims=True))
        weights = jnp.exp2((s - jnp.tile(m_new, (1, STEP // 128))) * SCALE)
        factor = jnp.exp2((m_old - m_new) * SCALE)
        part = weights[:, :128]
        for i in range(1, STEP // 128):
            part = part + weights[:, i * 128 : (i + 1) * 128]
        l[at, :] = l[at, :] * factor + part
        m[at, :] = m_new
        acc[at, :] = acc[at, :] * jnp.tile(factor, (1, LATENT // 128)) + jnp.dot(
            weights.astype(jnp.bfloat16),
            keys_of(j)[:, :LATENT],
            preferred_element_type=jnp.float32,
        )

    def after(g, j):
        done = g + 1 == groups
        return jnp.where(done, 0, g + 1), jnp.where(done, j + 1, j)

    @pl.when(steps > 0)
    def _():
        score(0, 0, even)

        def two(i, at):
            later = after(*at)
            score(*later, odd)
            gather(*at, even)
            at = after(*later)
            score(*at, even)
            gather(*later, odd)
            return at

        lax.fori_loop(0, steps * (groups // 2), two, (jnp.int32(0), jnp.int32(0)))

    if last:
        def give(g, carry):
            for head in range(GROUP):
                at = pl.ds(pl.multiple_of(g * rows + head * ROWS, ROWS), ROWS)
                total = jnp.sum(l[at, :], axis=1, keepdims=True)
                mixed = (acc[at, :] * (1.0 / total)).astype(jnp.bfloat16)
                out_ref[:, pl.ds(pl.multiple_of((g * GROUP + head) * VD, VD), VD)] = jnp.dot(
                    mixed, uv_ref[g * GROUP + head], preferred_element_type=jnp.float32
                ).astype(jnp.bfloat16)
            return carry

        lax.fori_loop(0, groups, give, 0)


def attend(scalars, queries, sets, offsets, state, w_uv):
    first, last = state is None, w_uv is not None
    n = len(sets)
    rows = GROUP * ROWS
    total = queries.shape[0]
    operands = [queries, *sets]
    if last:
        operands.append(w_uv)
    widths = (LATENT, 128, 128)
    aliases = {}
    if not first:
        if not last:
            aliases = {1 + len(operands) + i: i for i in range(len(widths))}
        operands += list(state)
    room = 8 * n + 2 * STEP // ROWS
    scratch = [
        pltpu.VMEM((room * ROWS, WIDTH), jnp.bfloat16),
        pltpu.SMEM((room,), jnp.int32),
        pltpu.SMEM((4,), jnp.int32),
        pltpu.VMEM((rows, STEP), jnp.float32),
        pltpu.VMEM((rows, STEP), jnp.float32),
    ]
    whole = pl.BlockSpec(memory_space=pltpu.VMEM)
    if last:
        out_shape = jax.ShapeDtypeStruct((ROWS, total // ROWS * VD), jnp.bfloat16)
        out_specs = whole
        scratch += [pltpu.VMEM((total, w), jnp.float32) for w in widths]
    else:
        out_shape = [jax.ShapeDtypeStruct((total, w), jnp.float32) for w in widths]
        out_specs = [whole] * len(widths)
    flops = 2 * total * 8 * n * ROWS * (WIDTH + LATENT)
    return pl.pallas_call(
        functools.partial(attend_kernel, offsets, first, last),
        out_shape=out_shape,
        in_specs=[pl.BlockSpec(memory_space=pltpu.SMEM)] + [whole] * len(operands),
        out_specs=out_specs,
        scratch_shapes=scratch,
        input_output_aliases=aliases,
        compiler_params=params(ATTEND_MIB),
        cost_estimate=pl.CostEstimate(
            flops=flops, transcendentals=total * 8 * n * ROWS, bytes_accessed=24 << 20
        ),
    )(scalars, *operands)


def cache_kernel(scalars, *refs):
    sets, (out_ref, buffer, sems) = refs[:8], refs[8:]
    me = scalars[3]
    x, z, y, c = me // 32, (me // 8) & 3, (me // 2) & 3, me & 1
    for slot in range(ROWS // BLOCK):
        group = scalars[4 + slot]
        block = group // 4
        dx, dz = (block // 32) ^ x, ((block // 8) - z) & 3
        dy, dc = ((block // 2) - y) & 3, (block & 1) ^ c
        row = (dz * 2 + dx) * ROWS + (group & 3) * BLOCK
        which = dc * 4 + dy
        for a in range(8):

            @pl.when(which == a)
            def _(a=a, row=row, slot=slot):
                pltpu.make_async_copy(
                    sets[a].at[pl.ds(pl.multiple_of(row, BLOCK), BLOCK), :],
                    buffer.at[slot * BLOCK : (slot + 1) * BLOCK, :],
                    sems.at[slot],
                ).start()

    for slot in range(ROWS // BLOCK):
        pltpu.make_async_copy(
            sets[0].at[:BLOCK, :],
            buffer.at[slot * BLOCK : (slot + 1) * BLOCK, :],
            sems.at[slot],
        ).wait()
    out_ref[...] = buffer[:, : LATENT + ROPE]


def cache_rows(scalars, sets):
    return pl.pallas_call(
        cache_kernel,
        out_shape=jax.ShapeDtypeStruct((ROWS, LATENT + ROPE), jnp.bfloat16),
        grid_spec=pltpu.PrefetchScalarGridSpec(
            num_scalar_prefetch=1,
            grid=(),
            in_specs=[pl.BlockSpec(memory_space=pl.ANY)] * 8,
            out_specs=pl.BlockSpec(memory_space=pltpu.VMEM),
            scratch_shapes=[
                pltpu.VMEM((ROWS, WIDTH), jnp.bfloat16),
                pltpu.SemaphoreType.DMA((ROWS // BLOCK,)),
            ],
        ),
        compiler_params=params(4),
        name="cache_rows",
    )(scalars, *sets)


def shard_of(x, z, y, c):
    return (x % 2) * 32 + (z % 4) * 8 + (y % 4) * 2 + c % 2


def fetch(array, dx=0, dz=0, dy=0, dc=0):
    everyone = [
        (x, z, y, c) for x in range(2) for z in range(4) for y in range(4) for c in range(2)
    ]
    pairs = [
        (shard_of(x + dx, z + dz, y + dy, c + dc), shard_of(x, z, y, c))
        for x, z, y, c in everyone
    ]
    return lax.ppermute(array, "seq", pairs)


def local(hidden, attn_gain, kv_down, kv_gain, q_nope, q_pe, w_uk, w_uv, doc_ids, slot_table):
    me = lax.axis_index("seq")
    positions = (me * ROWS + jnp.arange(ROWS, dtype=jnp.int32)).astype(jnp.float32)
    half = ROPE // 2
    frequency = jnp.exp(jnp.arange(half, dtype=jnp.float32) * (-2.0 * math.log(10000.0) / ROPE))
    angle = positions[:, None] * jnp.tile(frequency, 4)[None, :]
    sign = jnp.where((jnp.arange(128) & 63) < half, -1.0, 1.0).astype(jnp.float32)
    cosines, sines = jnp.cos(angle), jnp.sin(angle) * sign[None, :]

    starts = jnp.sum(
        (doc_ids[None, :] < jnp.arange(1, 4, dtype=jnp.int32)[:, None]).astype(jnp.int32), axis=1
    )
    slots = me * (ROWS // BLOCK) + jnp.arange(ROWS // BLOCK, dtype=jnp.int32)
    groups = jnp.arange(slot_table.shape[0], dtype=jnp.int32)
    held = jnp.sum(jnp.where(slot_table[None, :] == slots[:, None], groups[None, :], 0), axis=1)
    scalars = jnp.concatenate([starts, me[None].astype(jnp.int32), held])

    mine = project(hidden, attn_gain, kv_down)
    theirs = lax.ppermute(mine, "tensor", [(0, 1), (1, 0)])
    queries = make_queries(q_nope, q_pe, cosines, sines, w_uk)
    own = finish(mine, theirs, cosines, sines, kv_gain)

    two = jnp.concatenate([own, fetch(own, dx=1)], axis=0)
    eight = jnp.concatenate([two] + [fetch(two, dz=d) for d in (1, 2, 3)], axis=0)
    across = {0: eight}
    for d in (1, 3, 2):
        across[d] = fetch(eight, dy=d)
    beside = {d: fetch(across[d], dc=1) for d in (0, 1, 3, 2)}

    state = attend(
        scalars, queries, [across[0], beside[0]], [(0, 0), (0, 1)], None, None
    )
    state = attend(
        scalars,
        queries,
        [across[1], across[3], beside[1], beside[3]],
        [(1, 0), (3, 0), (1, 1), (3, 1)],
        state,
        None,
    )
    attn_values = attend(scalars, queries, [across[2], beside[2]], [(2, 0), (2, 1)], state, w_uv)
    latent_cache = cache_rows(
        scalars, [across[d] for d in range(4)] + [beside[d] for d in range(4)]
    )
    return attn_values, latent_cache


def solution(mesh):
    placed = (
        P("seq", "tensor"),
        P("tensor"),
        P("tensor", None),
        P(),
        P("seq", "tensor"),
        P("seq", "tensor"),
        P("tensor", None, None),
        P("tensor", None, None),
        P(),
        P(),
    )
    return jax.shard_map(
        local,
        mesh=mesh,
        in_specs=placed,
        out_specs=(P("seq", "tensor"), P("seq", None)),
        check_vma=False,
    )
```

```python
import functools
import math

import jax
import jax.numpy as jnp
from jax import lax
from jax.experimental import pallas as pl
from jax.experimental.pallas import tpu as pltpu
from jax.sharding import PartitionSpec as P


D = 7168
HEADS = 128
LATENT = 512
ROPE = 64
NOPE = 128
VD = 128
BLOCK = 16
WIDTH = 640

EPSILON = 1e-06
MASKED = -1e30
FLOOR = -1e20
SCALE = (NOPE + ROPE) ** (-0.5) * math.log2(math.e)

ROWS = 64
PACK = 8
GROUP = 16
STEP = 256
PARTS = 7
ATTEND_MIB = 14
COPY_STATE = False


def params(mib, **kw):
    return pltpu.CompilerParams(vmem_limit_bytes=mib << 20, **kw)


def swap_halves(x, lane):
    return jnp.where(
        (lane & 63) < 32, pltpu.roll(x, 96, axis=1), pltpu.roll(x, 32, axis=1)
    )


def project_kernel(hidden_hbm, gain_hbm, down_hbm, out_ref, hidden, gain, down, sems):
    tile = hidden.shape[1] // PARTS
    first = pltpu.make_async_copy(hidden_hbm, hidden, sems.at[PARTS])
    second = pltpu.make_async_copy(gain_hbm, gain, sems.at[PARTS + 1])
    first.start()
    second.start()
    parts = []
    for k in range(PARTS):
        columns = slice(k * tile, (k + 1) * tile)
        parts.append(
            pltpu.make_async_copy(
                down_hbm.at[:, columns], down.at[:, columns], sems.at[k]
            )
        )
        parts[-1].start()
    first.wait()
    second.wait()
    squares = jnp.zeros((ROWS, 1), jnp.float32)
    for k in range(PARTS):
        columns = slice(k * tile, (k + 1) * tile)
        widened = hidden[:, columns].astype(jnp.float32)
        normed = (widened * gain[columns].reshape(1, -1)).astype(jnp.bfloat16)
        squares = squares + jnp.sum(widened * widened, axis=1, keepdims=True)
        parts[k].wait()
        product = lax.dot_general(
            normed, down[:, columns], (((1,), (1,)), ((), ())), preferred_element_type=jnp.float32
        )
        if k == 0:
            out_ref[:, : LATENT + ROPE] = product
        else:
            out_ref[:, : LATENT + ROPE] += product
    out_ref[:, LATENT + ROPE :] = jnp.broadcast_to(squares, (ROWS, WIDTH - LATENT - ROPE))


def project(hidden, attn_gain, kv_down):
    width = hidden.shape[1]
    return pl.pallas_call(
        project_kernel,
        out_shape=jax.ShapeDtypeStruct((ROWS, WIDTH), jnp.float32),
        in_specs=[pl.BlockSpec(memory_space=pltpu.HBM)] * 3,
        out_specs=pl.BlockSpec(memory_space=pltpu.VMEM),
        scratch_shapes=[
            pltpu.VMEM((ROWS, width), jnp.bfloat16),
            pltpu.VMEM((width,), jnp.float32),
            pltpu.VMEM((LATENT + ROPE, width), jnp.bfloat16),
            pltpu.SemaphoreType.DMA((PARTS + 2,)),
        ],
        compiler_params=params(60),
        name="project",
    )(hidden, attn_gain, kv_down.T)


def finish_kernel(scalars, mine_ref, theirs_ref, cos_ref, sin_ref, gain_ref, out_ref):
    total = mine_ref[...] + theirs_ref[...]
    squares = total[:, WIDTH - 1 :]
    scaled = total * lax.rsqrt(squares / D + EPSILON)
    raw = scaled[:, :LATENT]
    mean = jnp.mean(raw * raw, axis=1, keepdims=True)
    latent = raw * lax.rsqrt(mean + EPSILON) * gain_ref[...]
    out_ref[:, :LATENT] = latent.astype(jnp.bfloat16)
    key = scaled[:, LATENT:]
    lane = lax.broadcasted_iota(jnp.int32, key.shape, 1)
    key = jnp.where(lane < ROPE, key, pltpu.roll(key, ROPE, axis=1))
    turned = key * cos_ref[...] + swap_halves(key, lane) * sin_ref[...]
    out_ref[:, LATENT:] = turned.astype(jnp.bfloat16)


def finish(scalars, mine, theirs, cosines, sines, kv_gain):
    return pl.pallas_call(
        finish_kernel,
        out_shape=jax.ShapeDtypeStruct((ROWS, WIDTH), jnp.bfloat16),
        in_specs=[pl.BlockSpec(memory_space=pltpu.SMEM)]
        + [pl.BlockSpec(memory_space=pltpu.VMEM)] * 5,
        compiler_params=params(4),
        name="finish",
    )(scalars, mine, theirs, cosines, sines, kv_gain.reshape(1, -1))


def join_kernel(*refs):
    parts, out_ref = refs[:-1], refs[-1]
    at = 0
    for part in parts:
        out_ref[at : at + part.shape[0], :] = part[...]
        at += part.shape[0]


def join(parts):
    return pl.pallas_call(
        join_kernel,
        out_shape=jax.ShapeDtypeStruct((sum(p.shape[0] for p in parts), WIDTH), jnp.bfloat16),
        compiler_params=params(4),
    )(*parts)


def queries_kernel(nope_ref, pe_ref, cos_ref, sin_ref, uk_ref, out_ref):
    lane = lax.broadcasted_iota(jnp.int32, (ROWS, 128), 1)
    for pair in range(PACK // 2):
        pe = pe_ref[:, pair * 128 : (pair + 1) * 128].astype(jnp.float32)
        turned = pe * cos_ref[...] + swap_halves(pe, lane) * sin_ref[...]
        for side in range(2):
            head = 2 * pair + side
            rows = slice(head * ROWS, (head + 1) * ROWS)
            keep = (lane < ROPE) if side == 0 else (lane >= ROPE)
            out_ref[rows, LATENT:] = jnp.where(keep, turned, 0.0).astype(jnp.bfloat16)
            out_ref[rows, :LATENT] = jnp.dot(
                nope_ref[:, head * NOPE : (head + 1) * NOPE],
                uk_ref[head],
                preferred_element_type=jnp.float32,
            ).astype(jnp.bfloat16)


def make_queries(q_nope, q_pe, cosines, sines, w_uk):
    heads = w_uk.shape[0]
    return pl.pallas_call(
        queries_kernel,
        out_shape=jax.ShapeDtypeStruct((heads * ROWS, WIDTH), jnp.bfloat16),
        grid=(heads // PACK,),
        in_specs=[
            pl.BlockSpec((ROWS, PACK * NOPE), lambda g: (0, g)),
            pl.BlockSpec((ROWS, PACK * ROPE), lambda g: (0, g)),
            pl.BlockSpec((ROWS, 128), lambda g: (0, 0)),
            pl.BlockSpec((ROWS, 128), lambda g: (0, 0)),
            pl.BlockSpec((PACK, NOPE, LATENT), lambda g: (g, 0, 0)),
        ],
        out_specs=pl.BlockSpec((PACK * ROWS, WIDTH), lambda g: (g, 0)),
        compiler_params=params(16, dimension_semantics=("arbitrary",)),
        name="queries",
    )(q_nope, q_pe, cosines, sines, w_uk)


def start_of(scalars, position):
    start = jnp.int32(0)
    for i in range(3):
        start = jnp.maximum(start, jnp.where(scalars[i] <= position, scalars[i], 0))
    return start


def attend_kernel(offsets, first, last, *refs):
    n = len(offsets)
    refs = list(refs)
    scalars = refs.pop(0)
    q_ref = refs.pop(0)
    sets = [refs.pop(0) for _ in range(n)]
    if last:
        uv_ref = refs.pop(0)
        others, refs = refs[:6], refs[6:]
    if not first:
        before, refs = refs[:3], refs[3:]
    acc, m, l = refs[:3]
    refs = refs[3:]
    if last:
        out_ref, cache_ref = refs[:2]
        refs = refs[2:]
    kv, ids, counts, even, odd = refs
    me = scalars[3]
    blocks = STEP // ROWS
    rows = GROUP * ROWS
    groups = q_ref.shape[0] // rows

    x, z, y, c = me // 32, (me // 8) & 3, (me // 2) & 3, me & 1
    lowest = start_of(scalars, me * ROWS)
    counts[0] = 0
    for a, (dy, dc) in enumerate(offsets):
        for b in range(8):
            dz, dx = b // 2, b % 2
            block = (x ^ dx) * 32 + ((z + dz) & 3) * 8 + ((y + dy) & 3) * 2 + (c ^ dc)
            needed = (block <= me) & (block * ROWS + ROWS - 1 >= lowest)

            @pl.when(needed)
            def _(a=a, b=b, block=block):
                at = counts[0]
                ids[at] = block
                kv[pl.ds(pl.multiple_of(at * ROWS, ROWS), ROWS), :] = sets[a][
                    b * ROWS : (b + 1) * ROWS, :
                ]
                counts[0] = at + 1

    found = counts[0]
    for i in range(blocks - 1):
        ids[found + i] = HEADS * 1024
        kv[pl.ds(pl.multiple_of((found + i) * ROWS, ROWS), ROWS), :] = jnp.zeros(
            (ROWS, WIDTH), jnp.bfloat16
        )
    steps = (found + blocks - 1) // blocks

    def ready(g, carry):
        at = pl.ds(pl.multiple_of(g * rows, rows), rows)
        if first:
            acc[at, :] = jnp.zeros((rows, LATENT), jnp.float32)
            m[at, :] = jnp.full((rows, 128), FLOOR, jnp.float32)
            l[at, :] = jnp.zeros((rows, 128), jnp.float32)
        else:
            for new, old in zip((acc, m, l), before):
                new[at, :] = old[at, :]
        return carry

    if first or COPY_STATE:
        lax.fori_loop(0, groups, ready, 0)

    def keys_of(j):
        return kv[pl.ds(pl.multiple_of(j * STEP, STEP), STEP), :]

    def score(g, j, into):
        into[...] = lax.dot_general(
            q_ref[pl.ds(pl.multiple_of(g * rows, rows), rows), :],
            keys_of(j),
            (((1,), (1,)), ((), ())),
            preferred_element_type=jnp.float32,
        )

    def gather(g, j, scores):
        at = pl.ds(pl.multiple_of(g * rows, rows), rows)
        lane = lax.broadcasted_iota(jnp.int32, (ROWS, STEP), 1)
        key_block = jnp.full((ROWS, STEP), ids[blocks * j], jnp.int32)
        for i in range(1, blocks):
            key_block = jnp.where(lane >= i * ROWS, ids[blocks * j + i], key_block)
        key_position = key_block * ROWS + (lane & (ROWS - 1))
        position = me * ROWS + lax.broadcasted_iota(jnp.int32, (ROWS, STEP), 0)
        allowed = (key_position <= position) & (key_position >= start_of(scalars, position))
        s = jnp.where(allowed[None], scores[...].reshape(GROUP, ROWS, STEP), MASKED)
        s = s.reshape(rows, STEP)
        m_old = m[at, :]
        m_new = jnp.maximum(m_old, jnp.max(s, axis=1, keepdims=True))
        weights = jnp.exp2((s - jnp.tile(m_new, (1, STEP // 128))) * SCALE)
        factor = jnp.exp2((m_old - m_new) * SCALE)
        part = weights[:, :128]
        for i in range(1, STEP // 128):
            part = part + weights[:, i * 128 : (i + 1) * 128]
        l[at, :] = l[at, :] * factor + part
        m[at, :] = m_new
        acc[at, :] = acc[at, :] * jnp.tile(factor, (1, LATENT // 128)) + jnp.dot(
            weights.astype(jnp.bfloat16),
            keys_of(j)[:, :LATENT],
            preferred_element_type=jnp.float32,
        )

    def after(g, j):
        done = g + 1 == groups
        return jnp.where(done, 0, g + 1), jnp.where(done, j + 1, j)

    @pl.when(steps > 0)
    def _():
        score(0, 0, even)

        def two(i, at):
            later = after(*at)
            score(*later, odd)
            gather(*at, even)
            at = after(*later)
            score(*at, even)
            gather(*later, odd)
            return at

        lax.fori_loop(0, steps * (groups // 2), two, (jnp.int32(0), jnp.int32(0)))

    if last:
        where = [(0, 0), (0, 1), (1, 0), (3, 0), (1, 1), (3, 1), (2, 0), (2, 1)]
        for slot in range(ROWS // BLOCK):
            group = scalars[4 + slot]
            block = group // 4
            dx, dz = (block // 32) ^ x, ((block // 8) - z) & 3
            dy, dc = ((block // 2) - y) & 3, (block & 1) ^ c
            row = pl.multiple_of((dz * 2 + dx) * ROWS + (group & 3) * BLOCK, BLOCK)
            for source, (oy, oc) in zip([*others, *sets], where):

                @pl.when((dy == oy) & (dc == oc))
                def _(source=source, row=row, slot=slot):
                    cache_ref[slot * BLOCK : (slot + 1) * BLOCK, :] = source[
                        pl.ds(row, BLOCK), :
                    ][:, : LATENT + ROPE]

        def give(g, carry):
            for head in range(GROUP):
                at = pl.ds(pl.multiple_of(g * rows + head * ROWS, ROWS), ROWS)
                total = jnp.sum(l[at, :], axis=1, keepdims=True)
                mixed = (acc[at, :] * (1.0 / total)).astype(jnp.bfloat16)
                out_ref[:, pl.ds(pl.multiple_of((g * GROUP + head) * VD, VD), VD)] = jnp.dot(
                    mixed, uv_ref[g * GROUP + head], preferred_element_type=jnp.float32
                ).astype(jnp.bfloat16)
            return carry

        lax.fori_loop(0, groups, give, 0)


def attend(scalars, queries, sets, offsets, state=None, w_uv=None, others=()):
    first, last = state is None, w_uv is not None
    n = len(sets)
    rows = GROUP * ROWS
    total = queries.shape[0]
    widths = (LATENT, 128, 128)
    operands = [queries, *sets]
    if last:
        operands += [w_uv, *others]
    aliases = {}
    if not first:
        aliases = {1 + len(operands) + i: i for i in range(len(widths))}
        operands += list(state)
    room = 8 * n + 2 * STEP // ROWS
    scratch = [
        pltpu.VMEM((room * ROWS, WIDTH), jnp.bfloat16),
        pltpu.SMEM((room,), jnp.int32),
        pltpu.SMEM((4,), jnp.int32),
        pltpu.VMEM((rows, STEP), jnp.float32),
        pltpu.VMEM((rows, STEP), jnp.float32),
    ]
    whole = pl.BlockSpec(memory_space=pltpu.VMEM)
    out_shape = [jax.ShapeDtypeStruct((total, w), jnp.float32) for w in widths]
    if last:
        out_shape += [
            jax.ShapeDtypeStruct((ROWS, total // ROWS * VD), jnp.bfloat16),
            jax.ShapeDtypeStruct((ROWS, LATENT + ROPE), jnp.bfloat16),
        ]
    flops = 2 * total * 8 * n * ROWS * (WIDTH + LATENT)
    out = pl.pallas_call(
        functools.partial(attend_kernel, offsets, first, last),
        out_shape=out_shape,
        in_specs=[pl.BlockSpec(memory_space=pltpu.SMEM)] + [whole] * len(operands),
        out_specs=[whole] * len(out_shape),
        scratch_shapes=scratch,
        input_output_aliases=aliases,
        compiler_params=params(ATTEND_MIB),
        cost_estimate=pl.CostEstimate(
            flops=flops, transcendentals=total * 8 * n * ROWS, bytes_accessed=24 << 20
        ),
    )(scalars, *operands)
    return out[3:] if last else out


def shard_of(x, z, y, c):
    return (x % 2) * 32 + (z % 4) * 8 + (y % 4) * 2 + c % 2


def fetch(array, dx=0, dz=0, dy=0, dc=0):
    everyone = [
        (x, z, y, c) for x in range(2) for z in range(4) for y in range(4) for c in range(2)
    ]
    pairs = [
        (shard_of(x + dx, z + dz, y + dy, c + dc), shard_of(x, z, y, c))
        for x, z, y, c in everyone
    ]
    return lax.ppermute(array, "seq", pairs)


def local(hidden, attn_gain, kv_down, kv_gain, q_nope, q_pe, w_uk, w_uv, doc_ids, slot_table):
    me = lax.axis_index("seq")
    positions = (me * ROWS + jnp.arange(ROWS, dtype=jnp.int32)).astype(jnp.float32)
    half = ROPE // 2
    frequency = jnp.exp(jnp.arange(half, dtype=jnp.float32) * (-2.0 * math.log(10000.0) / ROPE))
    angle = positions[:, None] * jnp.tile(frequency, 4)[None, :]
    sign = jnp.where((jnp.arange(128) & 63) < half, -1.0, 1.0).astype(jnp.float32)
    cosines, sines = jnp.cos(angle), jnp.sin(angle) * sign[None, :]

    starts = jnp.sum(
        (doc_ids[None, :] < jnp.arange(1, 4, dtype=jnp.int32)[:, None]).astype(jnp.int32), axis=1
    )
    slots = me * (ROWS // BLOCK) + jnp.arange(ROWS // BLOCK, dtype=jnp.int32)
    groups = jnp.arange(slot_table.shape[0], dtype=jnp.int32)
    held = jnp.sum(jnp.where(slot_table[None, :] == slots[:, None], groups[None, :], 0), axis=1)
    scalars = jnp.concatenate([starts, me[None].astype(jnp.int32), held])

    mine = project(hidden, attn_gain, kv_down)
    theirs = lax.ppermute(mine, "tensor", [(0, 1), (1, 0)])
    queries = make_queries(q_nope, q_pe, cosines, sines, w_uk)
    own = finish(scalars, mine, theirs, cosines, sines, kv_gain)

    two = join([own, fetch(own, dx=1)])
    eight = join([two] + [fetch(two, dz=d) for d in (1, 2, 3)])
    across = {0: eight}
    for d in (1, 3, 2):
        across[d] = fetch(eight, dy=d)
    beside = {d: fetch(across[d], dc=1) for d in (0, 1, 3, 2)}

    state = attend(scalars, queries, [across[0], beside[0]], [(0, 0), (0, 1)])
    state = attend(scalars, queries, [across[1], across[3]], [(1, 0), (3, 0)], state)
    state = attend(scalars, queries, [beside[1], beside[3]], [(1, 1), (3, 1)], state)
    attn_values, latent_cache = attend(
        scalars,
        queries,
        [across[2], beside[2]],
        [(2, 0), (2, 1)],
        state,
        w_uv,
        [across[0], beside[0], across[1], across[3], beside[1], beside[3]],
    )
    return attn_values, latent_cache


def solution(mesh):
    placed = (
        P("seq", "tensor"),
        P("tensor"),
        P("tensor", None),
        P(),
        P("seq", "tensor"),
        P("seq", "tensor"),
        P("tensor", None, None),
        P("tensor", None, None),
        P(),
        P(),
    )
    return jax.shard_map(
        local,
        mesh=mesh,
        in_specs=placed,
        out_specs=(P("seq", "tensor"), P("seq", None)),
        check_vma=False,
    )
```

```python
import functools
import math

import jax
import jax.numpy as jnp
from jax import lax
from jax.experimental import pallas as pl
from jax.experimental.pallas import tpu as pltpu
from jax.sharding import PartitionSpec as P


D = 7168
HEADS = 128
LATENT = 512
ROPE = 64
NOPE = 128
VD = 128
BLOCK = 16
WIDTH = 640

EPSILON = 1e-06
MASKED = -1e30
FLOOR = -1e20
SCALE = (NOPE + ROPE) ** (-0.5) * math.log2(math.e)

ROWS = 64
PACK = 8
GROUP = 16
STEP = 256
PARTS = 7
ATTEND_MIB = 10
WAIT = pl.CostEstimate(flops=5 * 10**9, transcendentals=0, bytes_accessed=1 << 20)
PLACE, LIST, BEFORE, SCALARS = 0, 64, 136, 208
SETS = ((0, 0), (0, 1), (1, 0), (3, 0), (1, 1), (3, 1), (2, 0), (2, 1))


def params(mib, **kw):
    return pltpu.CompilerParams(vmem_limit_bytes=mib << 20, **kw)


def swap_halves(x, lane):
    return jnp.where(
        (lane & 63) < 32, pltpu.roll(x, 96, axis=1), pltpu.roll(x, 32, axis=1)
    )


def project_kernel(hidden_hbm, gain_hbm, down_hbm, out_ref, hidden, gain, down, sems):
    tile = hidden.shape[1] // PARTS
    first = pltpu.make_async_copy(hidden_hbm, hidden, sems.at[PARTS])
    second = pltpu.make_async_copy(gain_hbm, gain, sems.at[PARTS + 1])
    first.start()
    second.start()
    parts = []
    for k in range(PARTS):
        columns = slice(k * tile, (k + 1) * tile)
        parts.append(
            pltpu.make_async_copy(
                down_hbm.at[:, columns], down.at[:, columns], sems.at[k]
            )
        )
        parts[-1].start()
    first.wait()
    second.wait()
    squares = jnp.zeros((ROWS, 1), jnp.float32)
    for k in range(PARTS):
        columns = slice(k * tile, (k + 1) * tile)
        widened = hidden[:, columns].astype(jnp.float32)
        normed = (widened * gain[columns].reshape(1, -1)).astype(jnp.bfloat16)
        squares = squares + jnp.sum(widened * widened, axis=1, keepdims=True)
        parts[k].wait()
        product = lax.dot_general(
            normed, down[:, columns], (((1,), (1,)), ((), ())), preferred_element_type=jnp.float32
        )
        if k == 0:
            out_ref[:, : LATENT + ROPE] = product
        else:
            out_ref[:, : LATENT + ROPE] += product
    out_ref[:, LATENT + ROPE :] = jnp.broadcast_to(squares, (ROWS, WIDTH - LATENT - ROPE))


def project(hidden, attn_gain, kv_down):
    width = hidden.shape[1]
    return pl.pallas_call(
        project_kernel,
        out_shape=jax.ShapeDtypeStruct((ROWS, WIDTH), jnp.float32),
        in_specs=[pl.BlockSpec(memory_space=pltpu.HBM)] * 3,
        out_specs=pl.BlockSpec(memory_space=pltpu.VMEM),
        scratch_shapes=[
            pltpu.VMEM((ROWS, width), jnp.bfloat16),
            pltpu.VMEM((width,), jnp.float32),
            pltpu.VMEM((LATENT + ROPE, width), jnp.bfloat16),
            pltpu.SemaphoreType.DMA((PARTS + 2,)),
        ],
        compiler_params=params(60),
        name="project",
    )(hidden, attn_gain, kv_down.T)


def finish_kernel(mine_ref, theirs_ref, cos_ref, sin_ref, gain_ref, out_ref):
    total = mine_ref[...] + theirs_ref[...]
    squares = total[:, WIDTH - 1 :]
    scaled = total * lax.rsqrt(squares / D + EPSILON)
    raw = scaled[:, :LATENT]
    mean = jnp.mean(raw * raw, axis=1, keepdims=True)
    latent = raw * lax.rsqrt(mean + EPSILON) * gain_ref[...].reshape(1, -1)
    out_ref[:, :LATENT] = latent.astype(jnp.bfloat16)
    key = scaled[:, LATENT:]
    lane = lax.broadcasted_iota(jnp.int32, key.shape, 1)
    key = jnp.where(lane < ROPE, key, pltpu.roll(key, ROPE, axis=1))
    turned = key * cos_ref[...] + swap_halves(key, lane) * sin_ref[...]
    out_ref[:, LATENT:] = turned.astype(jnp.bfloat16)


def finish(mine, theirs, cosines, sines, kv_gain):
    return pl.pallas_call(
        finish_kernel,
        out_shape=jax.ShapeDtypeStruct((ROWS, WIDTH), jnp.bfloat16),
        compiler_params=params(4),
        cost_estimate=WAIT,
        name="finish",
    )(mine, theirs, cosines, sines, kv_gain)


def join_kernel(*refs):
    parts, out_ref = refs[:-1], refs[-1]
    at = 0
    for part in parts:
        out_ref[at : at + part.shape[0], :] = part[...]
        at += part.shape[0]


def join(parts):
    return pl.pallas_call(
        join_kernel,
        out_shape=jax.ShapeDtypeStruct((sum(p.shape[0] for p in parts), WIDTH), jnp.bfloat16),
        compiler_params=params(4),
    )(*parts)


def keep_kernel(plan, mine_ref, gain_ref, mine_out, gain_out):
    mine_out[...] = mine_ref[...]
    gain_out[...] = gain_ref[...]


def keep(plan, mine, gain):
    return pl.pallas_call(
        keep_kernel,
        out_shape=[jax.ShapeDtypeStruct(a.shape, a.dtype) for a in (mine, gain)],
        in_specs=[pl.BlockSpec(memory_space=pltpu.SMEM)]
        + [pl.BlockSpec(memory_space=pltpu.VMEM)] * 2,
        out_specs=[pl.BlockSpec(memory_space=pltpu.VMEM)] * 2,
        compiler_params=params(4),
        cost_estimate=WAIT,
        name="keep",
    )(plan, mine, gain)


def blank_kernel(plan, acc, m, l):
    acc[...] = jnp.zeros_like(acc)
    m[...] = jnp.full_like(m, FLOOR)
    l[...] = jnp.zeros_like(l)


def blank(plan, rows):
    return pl.pallas_call(
        blank_kernel,
        out_shape=[jax.ShapeDtypeStruct((rows, w), jnp.float32) for w in (LATENT, 128, 128)],
        in_specs=[pl.BlockSpec(memory_space=pltpu.SMEM)],
        out_specs=[pl.BlockSpec(memory_space=pltpu.VMEM)] * 3,
        compiler_params=params(4),
        name="blank",
    )(plan)


def queries_kernel(nope_ref, pe_ref, cos_ref, sin_ref, uk_ref, out_ref):
    lane = lax.broadcasted_iota(jnp.int32, (ROWS, 128), 1)
    for pair in range(PACK // 2):
        pe = pe_ref[:, pair * 128 : (pair + 1) * 128].astype(jnp.float32)
        turned = pe * cos_ref[...] + swap_halves(pe, lane) * sin_ref[...]
        for side in range(2):
            head = 2 * pair + side
            rows = slice(head * ROWS, (head + 1) * ROWS)
            keep = (lane < ROPE) if side == 0 else (lane >= ROPE)
            out_ref[rows, LATENT:] = jnp.where(keep, turned, 0.0).astype(jnp.bfloat16)
            out_ref[rows, :LATENT] = jnp.dot(
                nope_ref[:, head * NOPE : (head + 1) * NOPE],
                uk_ref[head],
                preferred_element_type=jnp.float32,
            ).astype(jnp.bfloat16)


def make_queries(q_nope, q_pe, cosines, sines, w_uk):
    heads = w_uk.shape[0]
    return pl.pallas_call(
        queries_kernel,
        out_shape=jax.ShapeDtypeStruct((heads * ROWS, WIDTH), jnp.bfloat16),
        grid=(heads // PACK,),
        in_specs=[
            pl.BlockSpec((ROWS, PACK * NOPE), lambda g: (0, g)),
            pl.BlockSpec((ROWS, PACK * ROPE), lambda g: (0, g)),
            pl.BlockSpec((ROWS, 128), lambda g: (0, 0)),
            pl.BlockSpec((ROWS, 128), lambda g: (0, 0)),
            pl.BlockSpec((PACK, NOPE, LATENT), lambda g: (g, 0, 0)),
        ],
        out_specs=pl.BlockSpec((PACK * ROWS, WIDTH), lambda g: (g, 0)),
        compiler_params=params(16, dimension_semantics=("arbitrary",)),
        name="queries",
    )(q_nope, q_pe, cosines, sines, w_uk)


def make_plan(me, starts, held):
    x, z, y, c = me // 32, (me // 8) & 3, (me // 2) & 3, me & 1
    index = jnp.arange(64, dtype=jnp.int32)
    block = (
        (x ^ (index & 1)) * 32
        + ((z + (index // 2) % 4) & 3) * 8
        + ((y + jnp.repeat(jnp.array([s[0] for s in SETS], jnp.int32), 8)) & 3) * 2
        + (c ^ jnp.repeat(jnp.array([s[1] for s in SETS], jnp.int32), 8))
    )
    lowest = jnp.max(jnp.where(starts <= me * ROWS, starts, 0))
    needed = (block <= me) & (block * ROWS + ROWS - 1 >= lowest)
    upto = jnp.arange(72, dtype=jnp.int32)
    before = jnp.sum(jnp.where(index[None, :] < upto[:, None], needed[None, :], False), axis=1, dtype=jnp.int32)
    place = jnp.where(needed, before[:64], -1)
    listed = place[None, :] == upto[:, None]
    blocks = jnp.where(
        upto < before[64], jnp.sum(jnp.where(listed, block[None, :], 0), axis=1), HEADS * 1024
    )
    return jnp.concatenate([place, blocks, before, starts, me[None], held])


def plan_of(me, doc_ids, slot_table):
    starts = jnp.sum(
        (doc_ids[None, :] < jnp.arange(1, 4, dtype=jnp.int32)[:, None]).astype(jnp.int32), axis=1
    )
    slots = me * (ROWS // BLOCK) + jnp.arange(ROWS // BLOCK, dtype=jnp.int32)
    groups = jnp.arange(slot_table.shape[0], dtype=jnp.int32)
    held = jnp.sum(jnp.where(slot_table[None, :] == slots[:, None], groups[None, :], 0), axis=1)
    return make_plan(me, starts, held)


def start_of(plan, position):
    start = jnp.int32(0)
    for i in range(3):
        first = plan[SCALARS + i]
        start = jnp.maximum(start, jnp.where(first <= position, first, 0))
    return start


def attend_kernel(first_set, n, last, *refs):
    refs = list(refs)
    plan = refs.pop(0)
    q_ref = refs.pop(0)
    sets = [refs.pop(0) for _ in range(n)]
    if first_set:
        left = refs.pop(0)
    if last:
        uv_ref = refs.pop(0)
        others, refs = refs[:first_set], refs[first_set:]
    refs = refs[3:]
    acc, m, l = refs[:3]
    refs = refs[3:]
    if last:
        out_ref, cache_ref = refs[:2]
        refs = refs[2:]
    else:
        left_out = refs.pop(0)
    kv, even, odd = refs
    me = plan[SCALARS + 3]
    blocks = STEP // ROWS
    rows = GROUP * ROWS
    groups = q_ref.shape[0] // rows

    def rows_of(block):
        return pl.ds(pl.multiple_of(block * ROWS, ROWS), ROWS)

    base = plan[BEFORE + 8 * first_set] // blocks * blocks
    if first_set:
        for i in range(blocks - 1):
            kv[i * ROWS : (i + 1) * ROWS, :] = left[i * ROWS : (i + 1) * ROWS, :]
    for a in range(n):
        for b in range(8):
            place = plan[PLACE + (first_set + a) * 8 + b]

            @pl.when(place >= 0)
            def _(a=a, b=b, place=place):
                kv[rows_of(place - base), :] = sets[a][b * ROWS : (b + 1) * ROWS, :]

    found = plan[BEFORE + 8 * (first_set + n)] - base
    if last:
        steps = (found + blocks - 1) // blocks
        for i in range(blocks - 1):
            kv[rows_of(found + i), :] = jnp.zeros((ROWS, WIDTH), jnp.bfloat16)
    else:
        steps = found // blocks
        for i in range(blocks - 1):
            left_out[i * ROWS : (i + 1) * ROWS, :] = kv[rows_of(steps * blocks + i), :]

    def keys_of(j):
        return kv[pl.ds(pl.multiple_of(j * STEP, STEP), STEP), :]

    def score(g, j, into):
        into[...] = lax.dot_general(
            q_ref[pl.ds(pl.multiple_of(g * rows, rows), rows), :],
            keys_of(j),
            (((1,), (1,)), ((), ())),
            preferred_element_type=jnp.float32,
        )

    def gather(g, j, scores):
        at = pl.ds(pl.multiple_of(g * rows, rows), rows)
        lane = lax.broadcasted_iota(jnp.int32, (ROWS, STEP), 1)
        listed = LIST + base + blocks * j
        key_block = jnp.full((ROWS, STEP), plan[listed], jnp.int32)
        for i in range(1, blocks):
            key_block = jnp.where(lane >= i * ROWS, plan[listed + i], key_block)
        key_position = key_block * ROWS + (lane & (ROWS - 1))
        position = me * ROWS + lax.broadcasted_iota(jnp.int32, (ROWS, STEP), 0)
        allowed = (key_position <= position) & (key_position >= start_of(plan, position))
        s = jnp.where(allowed[None], scores[...].reshape(GROUP, ROWS, STEP), MASKED)
        s = s.reshape(rows, STEP)
        m_old = m[at, :]
        m_new = jnp.maximum(m_old, jnp.max(s, axis=1, keepdims=True))
        weights = jnp.exp2((s - jnp.tile(m_new, (1, STEP // 128))) * SCALE)
        factor = jnp.exp2((m_old - m_new) * SCALE)
        part = weights[:, :128]
        for i in range(1, STEP // 128):
            part = part + weights[:, i * 128 : (i + 1) * 128]
        l[at, :] = l[at, :] * factor + part
        m[at, :] = m_new
        acc[at, :] = acc[at, :] * jnp.tile(factor, (1, LATENT // 128)) + jnp.dot(
            weights.astype(jnp.bfloat16),
            keys_of(j)[:, :LATENT],
            preferred_element_type=jnp.float32,
        )

    def after(g, j):
        done = g + 1 == groups
        return jnp.where(done, 0, g + 1), jnp.where(done, j + 1, j)

    @pl.when(steps > 0)
    def _():
        score(0, 0, even)

        def two(i, at):
            later = after(*at)
            score(*later, odd)
            gather(*at, even)
            at = after(*later)
            score(*at, even)
            gather(*later, odd)
            return at

        lax.fori_loop(0, steps * (groups // 2), two, (jnp.int32(0), jnp.int32(0)))

    if last:
        x, z, y, c = me // 32, (me // 8) & 3, (me // 2) & 3, me & 1
        for slot in range(ROWS // BLOCK):
            group = plan[SCALARS + 4 + slot]
            block = group // 4
            dx, dz = (block // 32) ^ x, ((block // 8) - z) & 3
            dy, dc = ((block // 2) - y) & 3, (block & 1) ^ c
            row = pl.multiple_of((dz * 2 + dx) * ROWS + (group & 3) * BLOCK, BLOCK)
            for source, (oy, oc) in zip([*others, *sets], SETS):

                @pl.when((dy == oy) & (dc == oc))
                def _(source=source, row=row, slot=slot):
                    cache_ref[slot * BLOCK : (slot + 1) * BLOCK, :] = source[
                        pl.ds(row, BLOCK), :
                    ][:, : LATENT + ROPE]

        def give(g, carry):
            for head in range(GROUP):
                at = pl.ds(pl.multiple_of(g * rows + head * ROWS, ROWS), ROWS)
                total = jnp.sum(l[at, :], axis=1, keepdims=True)
                mixed = (acc[at, :] * (1.0 / total)).astype(jnp.bfloat16)
                out_ref[:, pl.ds(pl.multiple_of((g * GROUP + head) * VD, VD), VD)] = jnp.dot(
                    mixed, uv_ref[g * GROUP + head], preferred_element_type=jnp.float32
                ).astype(jnp.bfloat16)
            return carry

        lax.fori_loop(0, groups, give, 0)


def attend(plan, queries, sets, first_set, carried, w_uv=None, others=()):
    last = w_uv is not None
    *state, left = carried
    n = len(sets)
    rows = GROUP * ROWS
    total = queries.shape[0]
    widths = (LATENT, 128, 128)
    operands = [queries, *sets]
    if first_set:
        operands.append(left)
    if last:
        operands += [w_uv, *others]
    aliases = {1 + len(operands) + i: i for i in range(len(widths))}
    operands += list(state)
    room = (8 * n + 2 * STEP // ROWS) * ROWS
    scratch = [
        pltpu.VMEM((room, WIDTH), jnp.bfloat16),
        pltpu.VMEM((rows, STEP), jnp.float32),
        pltpu.VMEM((rows, STEP), jnp.float32),
    ]
    whole = pl.BlockSpec(memory_space=pltpu.VMEM)
    out_shape = [jax.ShapeDtypeStruct((total, w), jnp.float32) for w in widths]
    if last:
        out_shape += [
            jax.ShapeDtypeStruct((ROWS, total // ROWS * VD), jnp.bfloat16),
            jax.ShapeDtypeStruct((ROWS, LATENT + ROPE), jnp.bfloat16),
        ]
    else:
        out_shape.append(jax.ShapeDtypeStruct((STEP - ROWS, WIDTH), jnp.bfloat16))
    flops = 2 * total * 8 * n * ROWS * (WIDTH + LATENT)
    out = pl.pallas_call(
        functools.partial(attend_kernel, first_set, n, last),
        out_shape=out_shape,
        in_specs=[pl.BlockSpec(memory_space=pltpu.SMEM)] + [whole] * len(operands),
        out_specs=[whole] * len(out_shape),
        scratch_shapes=scratch,
        input_output_aliases=aliases,
        compiler_params=params(ATTEND_MIB),
        cost_estimate=pl.CostEstimate(
            flops=flops, transcendentals=total * 8 * n * ROWS, bytes_accessed=24 << 20
        ),
    )(plan, *operands)
    return out[3:] if last else out


def shard_of(x, z, y, c):
    return (x % 2) * 32 + (z % 4) * 8 + (y % 4) * 2 + c % 2


def fetch(array, dx=0, dz=0, dy=0, dc=0):
    everyone = [
        (x, z, y, c) for x in range(2) for z in range(4) for y in range(4) for c in range(2)
    ]
    pairs = [
        (shard_of(x + dx, z + dz, y + dy, c + dc), shard_of(x, z, y, c))
        for x, z, y, c in everyone
    ]
    return lax.ppermute(array, "seq", pairs)


def local(hidden, attn_gain, kv_down, kv_gain, q_nope, q_pe, w_uk, w_uv, doc_ids, slot_table):
    me = lax.axis_index("seq").astype(jnp.int32)
    positions = (me * ROWS + jnp.arange(ROWS, dtype=jnp.int32)).astype(jnp.float32)
    half = ROPE // 2
    frequency = jnp.exp(jnp.arange(half, dtype=jnp.float32) * (-2.0 * math.log(10000.0) / ROPE))
    angle = positions[:, None] * jnp.tile(frequency, 4)[None, :]
    sign = jnp.where((jnp.arange(128) & 63) < half, -1.0, 1.0).astype(jnp.float32)
    cosines, sines = jnp.cos(angle), jnp.sin(angle) * sign[None, :]

    plan = plan_of(me, doc_ids, slot_table)

    mine = project(hidden, attn_gain, kv_down)
    theirs = lax.ppermute(mine, "tensor", [(0, 1), (1, 0)])
    queries = make_queries(q_nope, q_pe, cosines, sines, w_uk)
    mine, kv_gain = keep(plan, mine, kv_gain)
    own = finish(mine, theirs, cosines, sines, kv_gain)
    state = blank(plan, queries.shape[0])

    two = join([own, fetch(own, dx=1)])
    eight = join([two] + [fetch(two, dz=d) for d in (1, 2, 3)])
    across = {0: eight}
    for d in (1, 3, 2):
        across[d] = fetch(eight, dy=d)
    beside = {d: fetch(across[d], dc=1) for d in (0, 1, 3, 2)}

    sets = [beside[dy] if dc else across[dy] for dy, dc in SETS]
    state = (*state, None)
    for at, n in ((0, 1), (1, 1), (2, 2), (4, 2), (6, 1)):
        state = attend(plan, queries, sets[at : at + n], at, state)
    attn_values, latent_cache = attend(
        plan, queries, sets[7:], 7, state, w_uv, sets[:7]
    )
    return attn_values, latent_cache


def solution(mesh):
    placed = (
        P("seq", "tensor"),
        P("tensor"),
        P("tensor", None),
        P(),
        P("seq", "tensor"),
        P("seq", "tensor"),
        P("tensor", None, None),
        P("tensor", None, None),
        P(),
        P(),
    )
    return jax.shard_map(
        local,
        mesh=mesh,
        in_specs=placed,
        out_specs=(P("seq", "tensor"), P("seq", None)),
        check_vma=False,
    )
```

```python
import functools
import math

import jax
import jax.numpy as jnp
from jax import lax
from jax.experimental import pallas as pl
from jax.experimental.pallas import tpu as pltpu
from jax.sharding import PartitionSpec as P


D = 7168
HEADS = 128
LATENT = 512
ROPE = 64
NOPE = 128
VD = 128
BLOCK = 16
WIDTH = 640

EPSILON = 1e-06
MASKED = -1e30
FLOOR = -1e20
SCALE = (NOPE + ROPE) ** (-0.5) * math.log2(math.e)

ROWS = 64
PACK = 8
GROUP = 16
STEP = 256
PARTS = 7
ATTEND_MIB = 10
WAIT = pl.CostEstimate(flops=5 * 10**9, transcendentals=0, bytes_accessed=1 << 20)
PLACE, LIST, DONE, SCALARS, LEFT = 0, 64, 136, 208, 7
SETS = ((0, 0), (0, 1), (1, 0), (3, 0), (1, 1), (3, 1), (2, 0), (2, 1))


def params(mib, **kw):
    return pltpu.CompilerParams(vmem_limit_bytes=mib << 20, **kw)


def swap_halves(x, lane):
    return jnp.where(
        (lane & 63) < 32, pltpu.roll(x, 96, axis=1), pltpu.roll(x, 32, axis=1)
    )


def project_kernel(hidden_hbm, gain_hbm, down_hbm, out_ref, hidden, gain, down, sems):
    tile = hidden.shape[1] // PARTS
    first = pltpu.make_async_copy(hidden_hbm, hidden, sems.at[PARTS])
    second = pltpu.make_async_copy(gain_hbm, gain, sems.at[PARTS + 1])
    first.start()
    second.start()
    parts = []
    for k in range(PARTS):
        columns = slice(k * tile, (k + 1) * tile)
        parts.append(
            pltpu.make_async_copy(
                down_hbm.at[:, columns], down.at[:, columns], sems.at[k]
            )
        )
        parts[-1].start()
    first.wait()
    second.wait()
    squares = jnp.zeros((ROWS, 1), jnp.float32)
    for k in range(PARTS):
        columns = slice(k * tile, (k + 1) * tile)
        widened = hidden[:, columns].astype(jnp.float32)
        normed = (widened * gain[columns].reshape(1, -1)).astype(jnp.bfloat16)
        squares = squares + jnp.sum(widened * widened, axis=1, keepdims=True)
        parts[k].wait()
        product = lax.dot_general(
            normed, down[:, columns], (((1,), (1,)), ((), ())), preferred_element_type=jnp.float32
        )
        if k == 0:
            out_ref[:, : LATENT + ROPE] = product
        else:
            out_ref[:, : LATENT + ROPE] += product
    out_ref[:, LATENT + ROPE :] = jnp.broadcast_to(squares, (ROWS, WIDTH - LATENT - ROPE))


def project(hidden, attn_gain, kv_down):
    width = hidden.shape[1]
    return pl.pallas_call(
        project_kernel,
        out_shape=jax.ShapeDtypeStruct((ROWS, WIDTH), jnp.float32),
        in_specs=[pl.BlockSpec(memory_space=pltpu.HBM)] * 3,
        out_specs=pl.BlockSpec(memory_space=pltpu.VMEM),
        scratch_shapes=[
            pltpu.VMEM((ROWS, width), jnp.bfloat16),
            pltpu.VMEM((width,), jnp.float32),
            pltpu.VMEM((LATENT + ROPE, width), jnp.bfloat16),
            pltpu.SemaphoreType.DMA((PARTS + 2,)),
        ],
        compiler_params=params(60),
        name="project",
    )(hidden, attn_gain, kv_down.T)


def finish_kernel(mine_ref, theirs_ref, cos_ref, sin_ref, gain_ref, out_ref):
    total = mine_ref[...] + theirs_ref[...]
    squares = total[:, WIDTH - 1 :]
    scaled = total * lax.rsqrt(squares / D + EPSILON)
    raw = scaled[:, :LATENT]
    mean = jnp.mean(raw * raw, axis=1, keepdims=True)
    latent = raw * lax.rsqrt(mean + EPSILON) * gain_ref[...].reshape(1, -1)
    out_ref[:, :LATENT] = latent.astype(jnp.bfloat16)
    key = scaled[:, LATENT:]
    lane = lax.broadcasted_iota(jnp.int32, key.shape, 1)
    key = jnp.where(lane < ROPE, key, pltpu.roll(key, ROPE, axis=1))
    turned = key * cos_ref[...] + swap_halves(key, lane) * sin_ref[...]
    out_ref[:, LATENT:] = turned.astype(jnp.bfloat16)


def finish(mine, theirs, cosines, sines, kv_gain):
    return pl.pallas_call(
        finish_kernel,
        out_shape=jax.ShapeDtypeStruct((ROWS, WIDTH), jnp.bfloat16),
        compiler_params=params(4),
        cost_estimate=WAIT,
        name="finish",
    )(mine, theirs, cosines, sines, kv_gain)


def join_kernel(*refs):
    parts, out_ref = refs[:-1], refs[-1]
    at = 0
    for part in parts:
        out_ref[at : at + part.shape[0], :] = part[...]
        at += part.shape[0]


def join(parts):
    return pl.pallas_call(
        join_kernel,
        out_shape=jax.ShapeDtypeStruct((sum(p.shape[0] for p in parts), WIDTH), jnp.bfloat16),
        compiler_params=params(4),
    )(*parts)


def keep_kernel(mine_ref, gain_ref, mine_out, gain_out):
    mine_out[...] = mine_ref[...]
    gain_out[...] = gain_ref[...]


def keep(mine, gain):
    return pl.pallas_call(
        keep_kernel,
        out_shape=[jax.ShapeDtypeStruct(a.shape, a.dtype) for a in (mine, gain)],
        in_specs=[pl.BlockSpec(memory_space=pltpu.VMEM)] * 2,
        out_specs=[pl.BlockSpec(memory_space=pltpu.VMEM)] * 2,
        compiler_params=params(4),
        cost_estimate=WAIT,
        name="keep",
    )(mine, gain)


def blank_kernel(plan, acc, m, l):
    acc[...] = jnp.zeros_like(acc)
    m[...] = jnp.full_like(m, FLOOR)
    l[...] = jnp.zeros_like(l)


def blank(plan, rows):
    return pl.pallas_call(
        blank_kernel,
        out_shape=[jax.ShapeDtypeStruct((rows, w), jnp.float32) for w in (LATENT, 128, 128)],
        in_specs=[pl.BlockSpec(memory_space=pltpu.SMEM)],
        out_specs=[pl.BlockSpec(memory_space=pltpu.VMEM)] * 3,
        compiler_params=params(4),
        name="blank",
    )(plan)


def queries_kernel(nope_ref, pe_ref, cos_ref, sin_ref, uk_ref, out_ref):
    lane = lax.broadcasted_iota(jnp.int32, (ROWS, 128), 1)
    for pair in range(PACK // 2):
        pe = pe_ref[:, pair * 128 : (pair + 1) * 128].astype(jnp.float32)
        turned = pe * cos_ref[...] + swap_halves(pe, lane) * sin_ref[...]
        for side in range(2):
            head = 2 * pair + side
            rows = slice(head * ROWS, (head + 1) * ROWS)
            keep = (lane < ROPE) if side == 0 else (lane >= ROPE)
            out_ref[rows, LATENT:] = jnp.where(keep, turned, 0.0).astype(jnp.bfloat16)
            out_ref[rows, :LATENT] = jnp.dot(
                nope_ref[:, head * NOPE : (head + 1) * NOPE],
                uk_ref[head],
                preferred_element_type=jnp.float32,
            ).astype(jnp.bfloat16)


def make_queries(q_nope, q_pe, cosines, sines, w_uk):
    heads = w_uk.shape[0]
    return pl.pallas_call(
        queries_kernel,
        out_shape=jax.ShapeDtypeStruct((heads * ROWS, WIDTH), jnp.bfloat16),
        grid=(heads // PACK,),
        in_specs=[
            pl.BlockSpec((ROWS, PACK * NOPE), lambda g: (0, g)),
            pl.BlockSpec((ROWS, PACK * ROPE), lambda g: (0, g)),
            pl.BlockSpec((ROWS, 128), lambda g: (0, 0)),
            pl.BlockSpec((ROWS, 128), lambda g: (0, 0)),
            pl.BlockSpec((PACK, NOPE, LATENT), lambda g: (g, 0, 0)),
        ],
        out_specs=pl.BlockSpec((PACK * ROWS, WIDTH), lambda g: (g, 0)),
        compiler_params=params(16, dimension_semantics=("arbitrary",)),
        name="queries",
    )(q_nope, q_pe, cosines, sines, w_uk)


def plan_kernel(me_ref, docs_ref, slots_ref, plan):
    me = me_ref[0]

    def count(mask, values):
        return jnp.sum(jnp.where(mask, values, 0.0), axis=1, keepdims=True)[0, 0].astype(jnp.int32)

    docs = docs_ref[...].reshape(1, -1)
    slots = slots_ref[...].reshape(1, -1)
    numbers = lax.broadcasted_iota(jnp.int32, slots.shape, 1).astype(jnp.float32)
    for i in range(3):
        plan[SCALARS + i] = count(docs <= i, jnp.ones(docs.shape, jnp.float32))
    plan[SCALARS + 3] = me
    for i in range(ROWS // BLOCK):
        plan[SCALARS + 4 + i] = count(slots == me * (ROWS // BLOCK) + i, numbers)
    for i in range(72):
        plan[LIST + i] = HEADS * 1024
    x, z, y, c = me // 32, (me // 8) & 3, (me // 2) & 3, me & 1
    lowest = start_of(plan, me * ROWS)
    other = me ^ 1
    lowest_there = start_of(plan, other * ROWS)
    mine, theirs = jnp.int32(0), jnp.int32(0)
    plan[DONE] = 0
    for a, (dy, dc) in enumerate(SETS):
        for b in range(8):
            dz, dx = b // 2, b % 2
            block = (x ^ dx) * 32 + ((z + dz) & 3) * 8 + ((y + dy) & 3) * 2 + (c ^ dc)
            needed = (block <= me) & (block * ROWS + ROWS - 1 >= lowest)
            plan[PLACE + 8 * a + b] = jnp.where(needed, mine, -1)
            plan[LIST + jnp.where(needed, mine, 71)] = block
            mine = mine + needed.astype(jnp.int32)
            block = block ^ 1
            there = (block <= other) & (block * ROWS + ROWS - 1 >= lowest_there)
            theirs = theirs + there.astype(jnp.int32)
        steps = mine // (STEP // ROWS)
        plan[DONE + 8 * (a + 1)] = jnp.maximum(
            jnp.minimum(steps, theirs // (STEP // ROWS)), steps - 1
        )
    plan[SCALARS + 8] = mine


def make_plan(me, doc_ids, slot_table):
    return pl.pallas_call(
        plan_kernel,
        out_shape=jax.ShapeDtypeStruct((224,), jnp.int32),
        in_specs=[pl.BlockSpec(memory_space=pltpu.SMEM)]
        + [pl.BlockSpec(memory_space=pltpu.VMEM)] * 2,
        out_specs=pl.BlockSpec(memory_space=pltpu.SMEM),
        compiler_params=params(4),
        name="plan",
    )(me[None], doc_ids, slot_table)


def start_of(plan, position):
    start = jnp.int32(0)
    for i in range(3):
        first = plan[SCALARS + i]
        start = jnp.maximum(start, jnp.where(first <= position, first, 0))
    return start


def attend_kernel(first_set, n, last, *refs):
    refs = list(refs)
    plan = refs.pop(0)
    q_ref = refs.pop(0)
    sets = [refs.pop(0) for _ in range(n)]
    if first_set:
        left = refs.pop(0)
    if last:
        uv_ref = refs.pop(0)
        others, refs = refs[:first_set], refs[first_set:]
    refs = refs[3:]
    acc, m, l = refs[:3]
    refs = refs[3:]
    if last:
        out_hbm, cache_ref = refs[:2]
        kv, even, odd, out_ref, sems = refs[2:]
    else:
        left_out = refs.pop(0)
        kv, even, odd = refs
    me = plan[SCALARS + 3]
    blocks = STEP // ROWS
    rows = GROUP * ROWS
    groups = q_ref.shape[0] // rows

    def rows_of(block):
        return pl.ds(pl.multiple_of(block * ROWS, ROWS), ROWS)

    before = jnp.maximum(plan[DONE + 8 * first_set], 0)
    base = before * blocks
    if first_set:
        for i in range(LEFT):
            kv[i * ROWS : (i + 1) * ROWS, :] = left[i * ROWS : (i + 1) * ROWS, :]
    for a in range(n):
        for b in range(8):
            place = plan[PLACE + (first_set + a) * 8 + b]

            @pl.when(place >= 0)
            def _(a=a, b=b, place=place):
                kv[rows_of(place - base), :] = sets[a][b * ROWS : (b + 1) * ROWS, :]

    if last:
        found = plan[SCALARS + 8] - base
        steps = (found + blocks - 1) // blocks
        for i in range(blocks - 1):
            kv[rows_of(found + i), :] = jnp.zeros((ROWS, WIDTH), jnp.bfloat16)
    else:
        steps = jnp.maximum(plan[DONE + 8 * (first_set + n)], 0) - before
        for i in range(LEFT):
            left_out[i * ROWS : (i + 1) * ROWS, :] = kv[rows_of(steps * blocks + i), :]

    def keys_of(j):
        return kv[pl.ds(pl.multiple_of(j * STEP, STEP), STEP), :]

    def score(g, j, into):
        into[...] = lax.dot_general(
            q_ref[pl.ds(pl.multiple_of(g * rows, rows), rows), :],
            keys_of(j),
            (((1,), (1,)), ((), ())),
            preferred_element_type=jnp.float32,
        )

    def gather(g, j, scores):
        at = pl.ds(pl.multiple_of(g * rows, rows), rows)
        lane = lax.broadcasted_iota(jnp.int32, (ROWS, STEP), 1)
        listed = LIST + base + blocks * j
        key_block = jnp.full((ROWS, STEP), plan[listed], jnp.int32)
        for i in range(1, blocks):
            key_block = jnp.where(lane >= i * ROWS, plan[listed + i], key_block)
        key_position = key_block * ROWS + (lane & (ROWS - 1))
        position = me * ROWS + lax.broadcasted_iota(jnp.int32, (ROWS, STEP), 0)
        allowed = (key_position <= position) & (key_position >= start_of(plan, position))
        s = jnp.where(allowed[None], scores[...].reshape(GROUP, ROWS, STEP), MASKED)
        s = s.reshape(rows, STEP)
        m_old = m[at, :]
        m_new = jnp.maximum(m_old, jnp.max(s, axis=1, keepdims=True))
        weights = jnp.exp2((s - jnp.tile(m_new, (1, STEP // 128))) * SCALE)
        factor = jnp.exp2((m_old - m_new) * SCALE)
        part = weights[:, :128]
        for i in range(1, STEP // 128):
            part = part + weights[:, i * 128 : (i + 1) * 128]
        l[at, :] = l[at, :] * factor + part
        m[at, :] = m_new
        acc[at, :] = acc[at, :] * jnp.tile(factor, (1, LATENT // 128)) + jnp.dot(
            weights.astype(jnp.bfloat16),
            keys_of(j)[:, :LATENT],
            preferred_element_type=jnp.float32,
        )

    def after(g, j):
        done = g + 1 == groups
        return jnp.where(done, 0, g + 1), jnp.where(done, j + 1, j)

    @pl.when(steps > 0)
    def _():
        score(0, 0, even)

        def two(i, at):
            later = after(*at)
            score(*later, odd)
            gather(*at, even)
            at = after(*later)
            score(*at, even)
            gather(*later, odd)
            return at

        lax.fori_loop(0, steps * (groups // 2), two, (jnp.int32(0), jnp.int32(0)))

    if last:
        x, z, y, c = me // 32, (me // 8) & 3, (me // 2) & 3, me & 1
        for slot in range(ROWS // BLOCK):
            group = plan[SCALARS + 4 + slot]
            block = group // 4
            dx, dz = (block // 32) ^ x, ((block // 8) - z) & 3
            dy, dc = ((block // 2) - y) & 3, (block & 1) ^ c
            row = pl.multiple_of((dz * 2 + dx) * ROWS + (group & 3) * BLOCK, BLOCK)
            for source, (oy, oc) in zip([*others, *sets], SETS):

                @pl.when((dy == oy) & (dc == oc))
                def _(source=source, row=row, slot=slot):
                    cache_ref[slot * BLOCK : (slot + 1) * BLOCK, :] = source[
                        pl.ds(row, BLOCK), :
                    ][:, : LATENT + ROPE]

        copies = []
        for g in range(groups):
            for head in range(g * GROUP, (g + 1) * GROUP):
                at = slice(head * ROWS, (head + 1) * ROWS)
                total = jnp.sum(l[at, :], axis=1, keepdims=True)
                mixed = (acc[at, :] * (1.0 / total)).astype(jnp.bfloat16)
                out_ref[:, head * VD : (head + 1) * VD] = jnp.dot(
                    mixed, uv_ref[head], preferred_element_type=jnp.float32
                ).astype(jnp.bfloat16)
            columns = slice(g * GROUP * VD, (g + 1) * GROUP * VD)
            copies.append(
                pltpu.make_async_copy(out_ref.at[:, columns], out_hbm.at[:, columns], sems.at[g])
            )
            copies[-1].start()
        for copy in copies:
            copy.wait()


def attend(plan, queries, sets, first_set, carried, w_uv=None, others=()):
    last = w_uv is not None
    *state, left = carried
    n = len(sets)
    rows = GROUP * ROWS
    total = queries.shape[0]
    widths = (LATENT, 128, 128)
    operands = [queries, *sets]
    if first_set:
        operands.append(left)
    if last:
        operands += [w_uv, *others]
    aliases = {1 + len(operands) + i: i for i in range(len(widths))}
    operands += list(state)
    room = (8 * n + 3 * STEP // ROWS) * ROWS
    scratch = [
        pltpu.VMEM((room, WIDTH), jnp.bfloat16),
        pltpu.VMEM((rows, STEP), jnp.float32),
        pltpu.VMEM((rows, STEP), jnp.float32),
    ]
    whole = pl.BlockSpec(memory_space=pltpu.VMEM)
    out_specs = [whole] * (len(widths) + 1)
    out_shape = [jax.ShapeDtypeStruct((total, w), jnp.float32) for w in widths]
    if last:
        out_shape += [
            jax.ShapeDtypeStruct((ROWS, total // ROWS * VD), jnp.bfloat16),
            jax.ShapeDtypeStruct((ROWS, LATENT + ROPE), jnp.bfloat16),
        ]
        out_specs[-1:] = [pl.BlockSpec(memory_space=pltpu.HBM), whole]
        scratch += [
            pltpu.VMEM((ROWS, total // ROWS * VD), jnp.bfloat16),
            pltpu.SemaphoreType.DMA((total // rows,)),
        ]
    else:
        out_shape.append(jax.ShapeDtypeStruct((LEFT * ROWS, WIDTH), jnp.bfloat16))
    flops = 2 * total * 8 * n * ROWS * (WIDTH + LATENT)
    out = pl.pallas_call(
        functools.partial(attend_kernel, first_set, n, last),
        out_shape=out_shape,
        in_specs=[pl.BlockSpec(memory_space=pltpu.SMEM)] + [whole] * len(operands),
        out_specs=out_specs,
        scratch_shapes=scratch,
        input_output_aliases=aliases,
        compiler_params=params(ATTEND_MIB),
        cost_estimate=pl.CostEstimate(
            flops=flops, transcendentals=total * 8 * n * ROWS, bytes_accessed=24 << 20
        ),
    )(plan, *operands)
    return out[3:] if last else out


def shard_of(x, z, y, c):
    return (x % 2) * 32 + (z % 4) * 8 + (y % 4) * 2 + c % 2


def fetch(array, dx=0, dz=0, dy=0, dc=0):
    everyone = [
        (x, z, y, c) for x in range(2) for z in range(4) for y in range(4) for c in range(2)
    ]
    pairs = [
        (shard_of(x + dx, z + dz, y + dy, c + dc), shard_of(x, z, y, c))
        for x, z, y, c in everyone
    ]
    return lax.ppermute(array, "seq", pairs)


def local(hidden, attn_gain, kv_down, kv_gain, q_nope, q_pe, w_uk, w_uv, doc_ids, slot_table):
    me = lax.axis_index("seq").astype(jnp.int32)
    positions = (me * ROWS + jnp.arange(ROWS, dtype=jnp.int32)).astype(jnp.float32)
    half = ROPE // 2
    frequency = jnp.exp(jnp.arange(half, dtype=jnp.float32) * (-2.0 * math.log(10000.0) / ROPE))
    angle = positions[:, None] * jnp.tile(frequency, 4)[None, :]
    sign = jnp.where((jnp.arange(128) & 63) < half, -1.0, 1.0).astype(jnp.float32)
    cosines, sines = jnp.cos(angle), jnp.sin(angle) * sign[None, :]

    mine = project(hidden, attn_gain, kv_down)
    theirs = lax.ppermute(mine, "tensor", [(0, 1), (1, 0)])
    queries = make_queries(q_nope, q_pe, cosines, sines, w_uk)
    mine, kv_gain = keep(mine, kv_gain)
    plan = make_plan(me, doc_ids, slot_table)
    own = finish(mine, theirs, cosines, sines, kv_gain)
    state = blank(plan, queries.shape[0])

    two = join([own, fetch(own, dx=1)])
    over_z = [fetch(two, dz=d) for d in (1, 2, 3)]
    early = {d: fetch(two, dy=d) for d in (1, 3)}
    six = join(over_z)
    late = {d: fetch(six, dy=d) for d in (1, 3)}
    eight = join([two, six])
    across = {0: eight, 2: fetch(eight, dy=2)}
    for d in (1, 3):
        across[d] = join([early[d], late[d]])
    beside = {d: fetch(across[d], dc=1) for d in (0, 1, 3, 2)}

    sets = [beside[dy] if dc else across[dy] for dy, dc in SETS]
    state = (*state, None)
    for at, n in ((0, 1), (1, 1), (2, 2), (4, 2), (6, 1)):
        state = attend(plan, queries, sets[at : at + n], at, state)
    attn_values, latent_cache = attend(
        plan, queries, sets[7:], 7, state, w_uv, sets[:7]
    )
    return attn_values, latent_cache


def solution(mesh):
    placed = (
        P("seq", "tensor"),
        P("tensor"),
        P("tensor", None),
        P(),
        P("seq", "tensor"),
        P("seq", "tensor"),
        P("tensor", None, None),
        P("tensor", None, None),
        P(),
        P(),
    )
    return jax.shard_map(
        local,
        mesh=mesh,
        in_specs=placed,
        out_specs=(P("seq", "tensor"), P("seq", None)),
        check_vma=False,
    )
```

```python
import functools
import math

import jax
import jax.numpy as jnp
from jax import lax
from jax.experimental import pallas as pl
from jax.experimental.pallas import tpu as pltpu
from jax.sharding import PartitionSpec as P


D = 7168
HEADS = 128
LATENT = 512
ROPE = 64
NOPE = 128
VD = 128
BLOCK = 16
WIDTH = 640

EPSILON = 1e-06
MASKED = -1e30
FLOOR = -1e20
SCALE = (NOPE + ROPE) ** (-0.5) * math.log2(math.e)

ROWS = 64
PACK = 8
GROUP = 16
STEP = 256
PARTS = 7
ATTEND_MIB = 10
WAIT = pl.CostEstimate(flops=5 * 10**9, transcendentals=0, bytes_accessed=1 << 20)
PLACE, LIST, DONE, SCALARS, LEFT = 0, 64, 136, 208, 7
SETS = ((0, 0), (0, 1), (1, 0), (3, 0), (1, 1), (3, 1), (2, 0), (2, 1))


def params(mib, **kw):
    return pltpu.CompilerParams(vmem_limit_bytes=mib << 20, **kw)


def swap_halves(x, lane):
    return jnp.where(
        (lane & 63) < 32, pltpu.roll(x, 96, axis=1), pltpu.roll(x, 32, axis=1)
    )


def project_kernel(hidden_hbm, gain_hbm, down_hbm, out_ref, hidden, gain, down, sems):
    tile = hidden.shape[1] // PARTS
    first = pltpu.make_async_copy(hidden_hbm, hidden, sems.at[PARTS])
    second = pltpu.make_async_copy(gain_hbm, gain, sems.at[PARTS + 1])
    first.start()
    second.start()
    parts = []
    for k in range(PARTS):
        columns = slice(k * tile, (k + 1) * tile)
        parts.append(
            pltpu.make_async_copy(
                down_hbm.at[:, columns], down.at[:, columns], sems.at[k]
            )
        )
        parts[-1].start()
    first.wait()
    second.wait()
    squares = jnp.zeros((ROWS, 1), jnp.float32)
    for k in range(PARTS):
        columns = slice(k * tile, (k + 1) * tile)
        widened = hidden[:, columns].astype(jnp.float32)
        normed = (widened * gain[columns].reshape(1, -1)).astype(jnp.bfloat16)
        squares = squares + jnp.sum(widened * widened, axis=1, keepdims=True)
        parts[k].wait()
        product = lax.dot_general(
            normed, down[:, columns], (((1,), (1,)), ((), ())), preferred_element_type=jnp.float32
        )
        if k == 0:
            out_ref[:, : LATENT + ROPE] = product
        else:
            out_ref[:, : LATENT + ROPE] += product
    out_ref[:, LATENT + ROPE :] = jnp.broadcast_to(squares, (ROWS, WIDTH - LATENT - ROPE))


def project(hidden, attn_gain, kv_down):
    width = hidden.shape[1]
    return pl.pallas_call(
        project_kernel,
        out_shape=jax.ShapeDtypeStruct((ROWS, WIDTH), jnp.float32),
        in_specs=[pl.BlockSpec(memory_space=pltpu.HBM)] * 3,
        out_specs=pl.BlockSpec(memory_space=pltpu.VMEM),
        scratch_shapes=[
            pltpu.VMEM((ROWS, width), jnp.bfloat16),
            pltpu.VMEM((width,), jnp.float32),
            pltpu.VMEM((LATENT + ROPE, width), jnp.bfloat16),
            pltpu.SemaphoreType.DMA((PARTS + 2,)),
        ],
        compiler_params=params(60),
        name="project",
    )(hidden, attn_gain, kv_down.T)


def finish_kernel(mine_ref, theirs_ref, cos_ref, sin_ref, gain_ref, out_ref):
    total = mine_ref[...] + theirs_ref[...]
    squares = total[:, WIDTH - 1 :]
    scaled = total * lax.rsqrt(squares / D + EPSILON)
    raw = scaled[:, :LATENT]
    mean = jnp.mean(raw * raw, axis=1, keepdims=True)
    latent = raw * lax.rsqrt(mean + EPSILON) * gain_ref[...].reshape(1, -1)
    out_ref[:, :LATENT] = latent.astype(jnp.bfloat16)
    key = scaled[:, LATENT:]
    lane = lax.broadcasted_iota(jnp.int32, key.shape, 1)
    key = jnp.where(lane < ROPE, key, pltpu.roll(key, ROPE, axis=1))
    turned = key * cos_ref[...] + swap_halves(key, lane) * sin_ref[...]
    out_ref[:, LATENT:] = turned.astype(jnp.bfloat16)


def finish(mine, theirs, cosines, sines, kv_gain):
    return pl.pallas_call(
        finish_kernel,
        out_shape=jax.ShapeDtypeStruct((ROWS, WIDTH), jnp.bfloat16),
        compiler_params=params(4),
        cost_estimate=WAIT,
        name="finish",
    )(mine, theirs, cosines, sines, kv_gain)


def join_kernel(*refs):
    parts, out_ref = refs[:-1], refs[-1]
    at = 0
    for part in parts:
        out_ref[at : at + part.shape[0], :] = part[...]
        at += part.shape[0]


def join(parts):
    return pl.pallas_call(
        join_kernel,
        out_shape=jax.ShapeDtypeStruct((sum(p.shape[0] for p in parts), WIDTH), jnp.bfloat16),
        compiler_params=params(4),
    )(*parts)


def keep_kernel(mine_ref, gain_ref, mine_out, gain_out):
    mine_out[...] = mine_ref[...]
    gain_out[...] = gain_ref[...]


def keep(mine, gain):
    return pl.pallas_call(
        keep_kernel,
        out_shape=[jax.ShapeDtypeStruct(a.shape, a.dtype) for a in (mine, gain)],
        in_specs=[pl.BlockSpec(memory_space=pltpu.VMEM)] * 2,
        out_specs=[pl.BlockSpec(memory_space=pltpu.VMEM)] * 2,
        compiler_params=params(4),
        cost_estimate=WAIT,
        name="keep",
    )(mine, gain)


def blank_kernel(acc, m, l):
    acc[...] = jnp.zeros_like(acc)
    m[...] = jnp.full_like(m, FLOOR)
    l[...] = jnp.zeros_like(l)


def blank(rows):
    return pl.pallas_call(
        blank_kernel,
        out_shape=[jax.ShapeDtypeStruct((rows, w), jnp.float32) for w in (LATENT, 128, 128)],
        out_specs=[pl.BlockSpec(memory_space=pltpu.VMEM)] * 3,
        compiler_params=params(4),
        name="blank",
    )()


def queries_kernel(nope_ref, pe_ref, cos_ref, sin_ref, uk_ref, out_ref):
    lane = lax.broadcasted_iota(jnp.int32, (ROWS, 128), 1)
    for pair in range(PACK // 2):
        pe = pe_ref[:, pair * 128 : (pair + 1) * 128].astype(jnp.float32)
        turned = pe * cos_ref[...] + swap_halves(pe, lane) * sin_ref[...]
        for side in range(2):
            head = 2 * pair + side
            rows = slice(head * ROWS, (head + 1) * ROWS)
            keep = (lane < ROPE) if side == 0 else (lane >= ROPE)
            out_ref[rows, LATENT:] = jnp.where(keep, turned, 0.0).astype(jnp.bfloat16)
            out_ref[rows, :LATENT] = jnp.dot(
                nope_ref[:, head * NOPE : (head + 1) * NOPE],
                uk_ref[head],
                preferred_element_type=jnp.float32,
            ).astype(jnp.bfloat16)


def make_queries(q_nope, q_pe, cosines, sines, w_uk):
    heads = w_uk.shape[0]
    return pl.pallas_call(
        queries_kernel,
        out_shape=jax.ShapeDtypeStruct((heads * ROWS, WIDTH), jnp.bfloat16),
        grid=(heads // PACK,),
        in_specs=[
            pl.BlockSpec((ROWS, PACK * NOPE), lambda g: (0, g)),
            pl.BlockSpec((ROWS, PACK * ROPE), lambda g: (0, g)),
            pl.BlockSpec((ROWS, 128), lambda g: (0, 0)),
            pl.BlockSpec((ROWS, 128), lambda g: (0, 0)),
            pl.BlockSpec((PACK, NOPE, LATENT), lambda g: (g, 0, 0)),
        ],
        out_specs=pl.BlockSpec((PACK * ROWS, WIDTH), lambda g: (g, 0)),
        compiler_params=params(16, dimension_semantics=("arbitrary",)),
        name="queries",
    )(q_nope, q_pe, cosines, sines, w_uk)


def plan_kernel(me_ref, docs_ref, slots_ref, plan):
    me = me_ref[0]

    def count(mask, values):
        return jnp.sum(jnp.where(mask, values, 0.0), axis=1, keepdims=True)[0, 0].astype(jnp.int32)

    docs = docs_ref[...].reshape(1, -1)
    slots = slots_ref[...].reshape(1, -1)
    numbers = lax.broadcasted_iota(jnp.int32, slots.shape, 1).astype(jnp.float32)
    for i in range(3):
        plan[SCALARS + i] = count(docs <= i, jnp.ones(docs.shape, jnp.float32))
    plan[SCALARS + 3] = me
    for i in range(ROWS // BLOCK):
        plan[SCALARS + 4 + i] = count(slots == me * (ROWS // BLOCK) + i, numbers)
    for i in range(72):
        plan[LIST + i] = HEADS * 1024
    x, z, y, c = me // 32, (me // 8) & 3, (me // 2) & 3, me & 1
    lowest = start_of(plan, me * ROWS)
    other = me ^ 1
    lowest_there = start_of(plan, other * ROWS)
    mine, theirs = jnp.int32(0), jnp.int32(0)
    plan[DONE] = 0
    for a, (dy, dc) in enumerate(SETS):
        for b in range(8):
            dz, dx = b // 2, b % 2
            block = (x ^ dx) * 32 + ((z + dz) & 3) * 8 + ((y + dy) & 3) * 2 + (c ^ dc)
            needed = (block <= me) & (block * ROWS + ROWS - 1 >= lowest)
            plan[PLACE + 8 * a + b] = jnp.where(needed, mine, -1)
            plan[LIST + jnp.where(needed, mine, 71)] = block
            mine = mine + needed.astype(jnp.int32)
            block = block ^ 1
            there = (block <= other) & (block * ROWS + ROWS - 1 >= lowest_there)
            theirs = theirs + there.astype(jnp.int32)
        steps = mine // (STEP // ROWS)
        plan[DONE + 8 * (a + 1)] = jnp.maximum(
            jnp.minimum(steps, theirs // (STEP // ROWS)), steps - 1
        )
    plan[SCALARS + 8] = mine


def make_plan(me, doc_ids, slot_table):
    return pl.pallas_call(
        plan_kernel,
        out_shape=jax.ShapeDtypeStruct((224,), jnp.int32),
        in_specs=[pl.BlockSpec(memory_space=pltpu.SMEM)]
        + [pl.BlockSpec(memory_space=pltpu.VMEM)] * 2,
        out_specs=pl.BlockSpec(memory_space=pltpu.SMEM),
        compiler_params=params(4),
        name="plan",
    )(me[None], doc_ids, slot_table)


def start_of(plan, position):
    start = jnp.int32(0)
    for i in range(3):
        first = plan[SCALARS + i]
        start = jnp.maximum(start, jnp.where(first <= position, first, 0))
    return start


def attend_kernel(first_set, n, last, *refs):
    refs = list(refs)
    plan = refs.pop(0)
    q_ref = refs.pop(0)
    sets = [refs.pop(0) for _ in range(n)]
    if first_set:
        left = refs.pop(0)
    if last:
        uv_ref = refs.pop(0)
        others, refs = refs[:first_set], refs[first_set:]
    refs = refs[3:]
    acc, m, l = refs[:3]
    refs = refs[3:]
    if last:
        out_hbm, cache_ref = refs[:2]
        kv, even, odd, out_ref, sems = refs[2:]
    else:
        left_out = refs.pop(0)
        kv, even, odd = refs
    me = plan[SCALARS + 3]
    blocks = STEP // ROWS
    rows = GROUP * ROWS
    groups = q_ref.shape[0] // rows

    def rows_of(block):
        return pl.ds(pl.multiple_of(block * ROWS, ROWS), ROWS)

    before = jnp.maximum(plan[DONE + 8 * first_set], 0)
    base = before * blocks
    if first_set:
        for i in range(LEFT):
            kv[i * ROWS : (i + 1) * ROWS, :] = left[i * ROWS : (i + 1) * ROWS, :]
    for a in range(n):
        for b in range(8):
            place = plan[PLACE + (first_set + a) * 8 + b]

            @pl.when(place >= 0)
            def _(a=a, b=b, place=place):
                kv[rows_of(place - base), :] = sets[a][b * ROWS : (b + 1) * ROWS, :]

    if last:
        found = plan[SCALARS + 8] - base
        steps = (found + blocks - 1) // blocks
        for i in range(blocks - 1):
            kv[rows_of(found + i), :] = jnp.zeros((ROWS, WIDTH), jnp.bfloat16)
    else:
        steps = jnp.maximum(plan[DONE + 8 * (first_set + n)], 0) - before
        for i in range(LEFT):
            left_out[i * ROWS : (i + 1) * ROWS, :] = kv[rows_of(steps * blocks + i), :]

    def keys_of(j):
        return kv[pl.ds(pl.multiple_of(j * STEP, STEP), STEP), :]

    def score(g, j, into):
        into[...] = lax.dot_general(
            q_ref[pl.ds(pl.multiple_of(g * rows, rows), rows), :],
            keys_of(j),
            (((1,), (1,)), ((), ())),
            preferred_element_type=jnp.float32,
        )

    def gather(g, j, scores):
        at = pl.ds(pl.multiple_of(g * rows, rows), rows)
        lane = lax.broadcasted_iota(jnp.int32, (ROWS, STEP), 1)
        listed = LIST + base + blocks * j
        key_block = jnp.full((ROWS, STEP), plan[listed], jnp.int32)
        for i in range(1, blocks):
            key_block = jnp.where(lane >= i * ROWS, plan[listed + i], key_block)
        key_position = key_block * ROWS + (lane & (ROWS - 1))
        position = me * ROWS + lax.broadcasted_iota(jnp.int32, (ROWS, STEP), 0)
        allowed = (key_position <= position) & (key_position >= start_of(plan, position))
        s = jnp.where(allowed[None], scores[...].reshape(GROUP, ROWS, STEP), MASKED)
        s = s.reshape(rows, STEP)
        m_old = m[at, :]
        m_new = jnp.maximum(m_old, jnp.max(s, axis=1, keepdims=True))
        weights = jnp.exp2((s - jnp.tile(m_new, (1, STEP // 128))) * SCALE)
        factor = jnp.exp2((m_old - m_new) * SCALE)
        part = weights[:, :128]
        for i in range(1, STEP // 128):
            part = part + weights[:, i * 128 : (i + 1) * 128]
        l[at, :] = l[at, :] * factor + part
        m[at, :] = m_new
        acc[at, :] = acc[at, :] * jnp.tile(factor, (1, LATENT // 128)) + jnp.dot(
            weights.astype(jnp.bfloat16),
            keys_of(j)[:, :LATENT],
            preferred_element_type=jnp.float32,
        )

    def after(g, j):
        done = g + 1 == groups
        return jnp.where(done, 0, g + 1), jnp.where(done, j + 1, j)

    @pl.when(steps > 0)
    def _():
        score(0, 0, even)

        def two(i, at):
            later = after(*at)
            score(*later, odd)
            gather(*at, even)
            at = after(*later)
            score(*at, even)
            gather(*later, odd)
            return at

        lax.fori_loop(0, steps * (groups // 2), two, (jnp.int32(0), jnp.int32(0)))

    if last:
        x, z, y, c = me // 32, (me // 8) & 3, (me // 2) & 3, me & 1
        for slot in range(ROWS // BLOCK):
            group = plan[SCALARS + 4 + slot]
            block = group // 4
            dx, dz = (block // 32) ^ x, ((block // 8) - z) & 3
            dy, dc = ((block // 2) - y) & 3, (block & 1) ^ c
            row = pl.multiple_of((dz * 2 + dx) * ROWS + (group & 3) * BLOCK, BLOCK)
            for source, (oy, oc) in zip([*others, *sets], SETS):

                @pl.when((dy == oy) & (dc == oc))
                def _(source=source, row=row, slot=slot):
                    cache_ref[slot * BLOCK : (slot + 1) * BLOCK, :] = source[
                        pl.ds(row, BLOCK), :
                    ][:, : LATENT + ROPE]

        copies = []
        for g in range(groups):
            for head in range(g * GROUP, (g + 1) * GROUP):
                at = slice(head * ROWS, (head + 1) * ROWS)
                total = jnp.sum(l[at, :], axis=1, keepdims=True)
                mixed = (acc[at, :] * (1.0 / total)).astype(jnp.bfloat16)
                out_ref[:, head * VD : (head + 1) * VD] = jnp.dot(
                    mixed, uv_ref[head], preferred_element_type=jnp.float32
                ).astype(jnp.bfloat16)
            columns = slice(g * GROUP * VD, (g + 1) * GROUP * VD)
            copies.append(
                pltpu.make_async_copy(out_ref.at[:, columns], out_hbm.at[:, columns], sems.at[g])
            )
            copies[-1].start()
        for copy in copies:
            copy.wait()


def attend(plan, queries, sets, first_set, carried, w_uv=None, others=()):
    last = w_uv is not None
    *state, left = carried
    n = len(sets)
    rows = GROUP * ROWS
    total = queries.shape[0]
    widths = (LATENT, 128, 128)
    operands = [queries, *sets]
    if first_set:
        operands.append(left)
    if last:
        operands += [w_uv, *others]
    aliases = {1 + len(operands) + i: i for i in range(len(widths))}
    operands += list(state)
    room = (8 * n + 3 * STEP // ROWS) * ROWS
    scratch = [
        pltpu.VMEM((room, WIDTH), jnp.bfloat16),
        pltpu.VMEM((rows, STEP), jnp.float32),
        pltpu.VMEM((rows, STEP), jnp.float32),
    ]
    whole = pl.BlockSpec(memory_space=pltpu.VMEM)
    out_specs = [whole] * (len(widths) + 1)
    out_shape = [jax.ShapeDtypeStruct((total, w), jnp.float32) for w in widths]
    if last:
        out_shape += [
            jax.ShapeDtypeStruct((ROWS, total // ROWS * VD), jnp.bfloat16),
            jax.ShapeDtypeStruct((ROWS, LATENT + ROPE), jnp.bfloat16),
        ]
        out_specs[-1:] = [pl.BlockSpec(memory_space=pltpu.HBM), whole]
        scratch += [
            pltpu.VMEM((ROWS, total // ROWS * VD), jnp.bfloat16),
            pltpu.SemaphoreType.DMA((total // rows,)),
        ]
    else:
        out_shape.append(jax.ShapeDtypeStruct((LEFT * ROWS, WIDTH), jnp.bfloat16))
    flops = 2 * total * 8 * n * ROWS * (WIDTH + LATENT)
    out = pl.pallas_call(
        functools.partial(attend_kernel, first_set, n, last),
        out_shape=out_shape,
        in_specs=[pl.BlockSpec(memory_space=pltpu.SMEM)] + [whole] * len(operands),
        out_specs=out_specs,
        scratch_shapes=scratch,
        input_output_aliases=aliases,
        compiler_params=params(ATTEND_MIB),
        cost_estimate=pl.CostEstimate(
            flops=flops, transcendentals=total * 8 * n * ROWS, bytes_accessed=24 << 20
        ),
    )(plan, *operands)
    return out[3:] if last else out


def shard_of(x, z, y, c):
    return (x % 2) * 32 + (z % 4) * 8 + (y % 4) * 2 + c % 2


def fetch(array, dx=0, dz=0, dy=0, dc=0):
    everyone = [
        (x, z, y, c) for x in range(2) for z in range(4) for y in range(4) for c in range(2)
    ]
    pairs = [
        (shard_of(x + dx, z + dz, y + dy, c + dc), shard_of(x, z, y, c))
        for x, z, y, c in everyone
    ]
    return lax.ppermute(array, "seq", pairs)


def local(hidden, attn_gain, kv_down, kv_gain, q_nope, q_pe, w_uk, w_uv, doc_ids, slot_table):
    me = lax.axis_index("seq").astype(jnp.int32)
    positions = (me * ROWS + jnp.arange(ROWS, dtype=jnp.int32)).astype(jnp.float32)
    half = ROPE // 2
    frequency = jnp.exp(jnp.arange(half, dtype=jnp.float32) * (-2.0 * math.log(10000.0) / ROPE))
    angle = positions[:, None] * jnp.tile(frequency, 4)[None, :]
    sign = jnp.where((jnp.arange(128) & 63) < half, -1.0, 1.0).astype(jnp.float32)
    cosines, sines = jnp.cos(angle), jnp.sin(angle) * sign[None, :]

    mine = project(hidden, attn_gain, kv_down)
    theirs = lax.ppermute(mine, "tensor", [(0, 1), (1, 0)])
    queries = make_queries(q_nope, q_pe, cosines, sines, w_uk)
    mine, kv_gain = keep(mine, kv_gain)
    plan = make_plan(me, doc_ids, slot_table)
    own = finish(mine, theirs, cosines, sines, kv_gain)
    state = blank(queries.shape[0])

    two = join([own, fetch(own, dx=1)])
    over_z = [fetch(two, dz=d) for d in (1, 2, 3)]
    early = {d: fetch(two, dy=d) for d in (1, 3)}
    six = join(over_z)
    late = {d: fetch(six, dy=d) for d in (1, 3)}
    eight = join([two, six])
    across = {0: eight, 2: fetch(eight, dy=2)}
    for d in (1, 3):
        across[d] = join([early[d], late[d]])
    beside = {d: fetch(across[d], dc=1) for d in (0, 1, 3, 2)}

    sets = [beside[dy] if dc else across[dy] for dy, dc in SETS]
    state = (*state, None)
    for at, n in ((0, 1), (1, 1), (2, 2), (4, 2), (6, 1)):
        state = attend(plan, queries, sets[at : at + n], at, state)
    attn_values, latent_cache = attend(
        plan, queries, sets[7:], 7, state, w_uv, sets[:7]
    )
    return attn_values, latent_cache


def solution(mesh):
    placed = (
        P("seq", "tensor"),
        P("tensor"),
        P("tensor", None),
        P(),
        P("seq", "tensor"),
        P("seq", "tensor"),
        P("tensor", None, None),
        P("tensor", None, None),
        P(),
        P(),
    )
    return jax.shard_map(
        local,
        mesh=mesh,
        in_specs=placed,
        out_specs=(P("seq", "tensor"), P("seq", None)),
        check_vma=False,
    )
```
